32 devices in a mesh: orb: 16 (over z, x, core), tm: 2 (over y).
Axes of the slice: x: 2, y: 2, z: 4, core: 2. Of those that a mesh axis runs over, the one named last changes fastest.
Arguments:
- integrals: bfloat16 [2048, 128, 128], P('orb'), may hold values from -6 to 6
- block_map: int32 [128, 4], P('orb'), may hold values 0 or 1
- green_occ: bfloat16 [2, 2048, 384], P('tm', 'orb'), may hold values from -0.5 to 0.5
- green_virt: bfloat16 [2, 2048, 384], P('tm', 'orb'), may hold values from -0.5 to 0.5
- coulomb: bfloat16 [2048, 512], P('orb'), may hold values from -0.0048828125 to 0.0048828125
- cosine: float32 [2, 2], replicated, may hold values from -1 to 1
Outputs:
- spectrum: float32 [2, 2048, 512], P('tm', 'orb')
The draws below stay inside these ranges and needn't reach their ends.
All inputs are finite; a program needn't handle non-finite values. No bound on the sum of `block_map` on one device may be relied on, other than what follows from the above.
Results may differ from the reference program's by a relative error of at most 0.0057.
Values may be sent and summed in bfloat16 or wider, within the bound.
A program may use at most 128 MiB of HBM per device.

```python
import jax
import jax.numpy as jnp
from jax import lax

ORB_DEV = 128
KW = 512
MCOL = 32
BLOCK = 16
AUX_DEV = 128
DOMAINS = 16
NORB = 2048
AUX = 2048
TIMES = 2
FREQS = 2


def place_ends(result, rng, low, largest):
    index_at = [jax.random.randint(jax.random.fold_in(rng, axis), (), 0, length) for axis, length in enumerate(result.shape)]
    main_axis = result.shape.index(max(result.shape))
    beside = index_at[:main_axis] + [(index_at[main_axis] + 1) % result.shape[main_axis]] + index_at[main_axis + 1:]
    return result.at[tuple(index_at)].set(low).at[tuple(beside)].set(largest)


def levels(own_key, shape, pieces, least, high):
    def one(position, blocks):
        heights = jax.random.uniform(jax.random.fold_in(jax.random.fold_in(own_key, 6), position), (blocks,), jnp.float32, least / len(pieces), high / len(pieces))
        return jnp.repeat(jnp.exp(heights), shape[position] // blocks).reshape((-1,) + (1,) * (len(shape) - position - 1))

    gain = one(*pieces[0])
    for cut in pieces[1:]:
        gain = gain * one(*cut)
    return gain


def bell_draw(own_key, extent, deviation, most, pieces=(), held_as=jnp.bfloat16):
    result = deviation * jax.random.normal(own_key, extent, jnp.float32)
    if pieces:
        result = result * levels(own_key, extent, pieces, -0.22, 0.18)
    return jnp.clip(result, -most, most).astype(held_as)


def setup_inputs(seed: int = 0) -> dict:
    keys = jax.random.split(jax.random.key(seed), 7)
    integrals = bell_draw(keys[0], (AUX, ORB_DEV, ORB_DEV), 1.0, 6.0, ((0, 16),))
    block_map = place_ends((jax.random.randint(keys[1], (AUX // BLOCK, ORB_DEV // MCOL), 0, 2) < 1).astype(jnp.int32), jax.random.fold_in(keys[1], 1), 0, 1)
    green_occ = bell_draw(keys[2], (TIMES, NORB, 3 * ORB_DEV), ORB_DEV ** -0.5, 0.5, ((0, 2), (1, 16)))
    green_virt = bell_draw(keys[3], (TIMES, NORB, 3 * ORB_DEV), ORB_DEV ** -0.5, 0.5, ((0, 2), (1, 16)))
    coulomb = bell_draw(keys[4], (AUX, KW), (3 * AUX_DEV * ORB_DEV * ORB_DEV // 4) ** -0.5, 0.0048828125, ((0, 16),))
    cosine = jnp.clip(jax.random.uniform(keys[5], (FREQS, TIMES), jnp.float32, -1.0, 1.0), -1.0, 1.0)
    return {"integrals": integrals, "block_map": block_map, "green_occ": green_occ, "green_virt": green_virt, "coulomb": coulomb, "cosine": cosine}


def reference(integrals, block_map, green_occ, green_virt, coulomb, cosine):
    keep_mask = block_map.astype(jnp.bfloat16)[:, None, :, None, None]
    shaped = integrals.reshape(AUX // BLOCK, BLOCK, ORB_DEV // MCOL, MCOL, ORB_DEV)
    masked = (shaped * keep_mask).reshape(DOMAINS, AUX_DEV, ORB_DEV, ORB_DEV)
    occ_tiles = green_occ.reshape(TIMES, DOMAINS, ORB_DEV, 3, ORB_DEV)
    virt_tiles = green_virt.reshape(TIMES, DOMAINS, ORB_DEV, 3, ORB_DEV)
    coulomb_rows = coulomb.reshape(DOMAINS, AUX_DEV, KW)
    pair_count = ORB_DEV * ORB_DEV

    def one_time(tile_pair):
        occ_time, virt_time = tile_pair

        def one_domain(domain_index):
            own_flat = masked[domain_index].reshape(AUX_DEV, pair_count)
            running_sum = jnp.zeros((AUX_DEV, KW), jnp.float32)
            for offset in range(3):
                neighbor_index = (domain_index + offset - 1) % DOMAINS
                source = masked[neighbor_index].astype(jnp.float32)
                occ_tile = occ_time[domain_index, :, offset, :].astype(jnp.float32)
                virt_tile = virt_time[domain_index, :, offset, :].astype(jnp.float32)
                half_side = jnp.einsum("qls,ns->qln", source, virt_tile).astype(jnp.bfloat16)
                pair_side = jnp.einsum("ml,qln->qmn", occ_tile, half_side.astype(jnp.float32)).astype(jnp.bfloat16)
                response = lax.dot_general(own_flat, pair_side.reshape(AUX_DEV, pair_count), (((1,), (1,)), ((), ())), preferred_element_type=jnp.float32).astype(jnp.bfloat16)
                running_sum = running_sum + jnp.dot(response, coulomb_rows[neighbor_index], preferred_element_type=jnp.float32)
            return running_sum.astype(jnp.bfloat16)

        return lax.map(one_domain, jnp.arange(DOMAINS, dtype=jnp.int32))

    panels = lax.map(one_time, (occ_tiles, virt_tiles)).reshape(TIMES, AUX, KW)
    return jnp.einsum("ft,tpk->fpk", cosine, panels.astype(jnp.float32), precision=lax.Precision.HIGHEST)
```

```python
import functools

import jax
import jax.numpy as jnp
from jax import lax
from jax.experimental import pallas as pl
from jax.experimental.pallas import tpu as pltpu
from jax.sharding import PartitionSpec as P

MESH = pl.DeviceIdType.MESH
BF = jnp.bfloat16
F32 = jnp.float32


def mm(a, b):
    return jnp.dot(a, b, preferred_element_type=F32)


def mm_nt(a, b):
    return lax.dot_general(a, b, (((1,), (1,)), ((), ())), preferred_element_type=F32)


def mm_tn(a, b):
    return lax.dot_general(a, b, (((0,), (0,)), ((), ())), preferred_element_type=F32)


def flip(tile):
    return tile.astype(F32).T.astype(BF)


def lay(parts):
    return parts[0] if len(parts) == 1 else jnp.concatenate(parts, axis=1)


def plan(orb, step):
    cuts = [(i * step, step) for i in range(orb // step - 1)]
    last = orb - step
    half = step // 2
    return cuts + [(last, half), (last + half, half)]


def kernel(
    chain, times, batch, step,
    ints, bmap, occ, virt, coul, cosine, out,
    own, own_rel, xbuf, side, diag_rel, stage, bm, mask, cos,
    occ_prev, occ_own, occ_edge, virt_prev, virt_own, virt_edge,
    l_prev, w_prev, w_own, w_edge, coul_own, coul_left, coul_right,
    acc, acc_diag, z_send, z_recv,
    load_sem, own_sem, x_send, x_recv, edge_send, edge_recv, tile_send, tile_recv,
    coul_send, coul_recv, pass_send, pass_recv, zs_send, zs_recv,
):
    aux, orb = ints.shape[0], ints.shape[1]
    part = aux // times
    col_blocks, row_blocks = bmap.shape
    width = orb // col_blocks
    group = aux // row_blocks
    me = lax.axis_index("orb")
    y = lax.axis_index("tm")
    right = lax.rem(me + 1, chain)
    left = lax.rem(me + chain - 1, chain)
    later = [lax.rem(y + d, times) for d in range(times)]
    before = [lax.rem(y + times - d, times) for d in range(times)]

    barrier = pltpu.get_barrier_semaphore()
    for d in range(times):
        for where in (left, right) + ((me,) if d else ()):
            pl.semaphore_signal(
                barrier, inc=1, device_id=(where, later[d]), device_id_type=MESH
            )

    def load(src, dst, sem):
        copy = pltpu.make_async_copy(src, dst, sem)
        copy.start()
        return copy

    mine = pl.multiple_of(y * part, part)
    map_load = load(bmap, bm, load_sem.at[0])
    own_loads = []
    for d in range(times):
        rows = pl.ds(pl.multiple_of(later[d] * part, part), part)
        own_loads.append(load(ints.at[rows], own.at[rows], own_sem.at[d]))
    tile_loads = []
    for k, (src, prev, mid) in enumerate(
        ((occ, occ_prev, occ_own), (virt, virt_prev, virt_own))
    ):
        tile_loads.append(load(src.at[0, :, pl.ds(0, orb)], prev.at[0], load_sem.at[1 + k]))
        tile_loads.append(load(src.at[0, :, pl.ds(orb, orb)], mid.at[0], load_sem.at[3 + k]))
    late_loads = [load(coul, coul_own, load_sem.at[5]), load(cosine, cos, load_sem.at[6])]

    pl.semaphore_wait(barrier, 3 * times - 1)

    def remote(src, dst, s, r, where, peer):
        return pltpu.make_async_remote_copy(
            src_ref=src, dst_ref=dst, send_sem=s, recv_sem=r,
            device_id=(where, peer), device_id_type=MESH,
        )

    def send(*args):
        copy = remote(*args)
        copy.start()
        return copy

    edges = []
    for k, (src, dst) in enumerate(((occ, occ_edge), (virt, virt_edge))):
        edges.append(send(
            src.at[0, :, pl.ds(2 * orb, orb)], dst.at[0],
            edge_send.at[0, k], edge_recv.at[0, k], right, y,
        ))
    tiles = []
    for d in range(1, times):
        for k, (src, dst, place) in enumerate((
            (occ, occ_own, 1), (virt, virt_own, 1), (occ, occ_prev, 0), (virt, virt_prev, 0),
        )):
            tiles.append(send(
                src.at[0, :, pl.ds(place * orb, orb)], dst.at[d],
                tile_send.at[d, k], tile_recv.at[d, k], me, before[d],
            ))

    map_load.wait()
    values = bm[...].astype(F32)
    for r in range(row_blocks):
        for c in range(col_blocks):
            mask[r, pl.ds(c * width, width), :] = jnp.broadcast_to(
                values[c : c + 1, r : r + 1], (width, orb)
            ).astype(BF)

    def arrange(first, block):
        rows = pl.ds(pl.multiple_of(block, step), step)
        for g in range(part // group):
            at = pl.multiple_of(first + g * group, group)
            tile = own[pl.ds(at, group), rows, :] * mask[at // group, rows, :][None]
            own_rel[rows, pl.ds(at, group), :] = jnp.swapaxes(tile, 0, 1)

    slices = plan(orb, step)
    full = orb // step - 1

    def piece(start, length, i):
        rows = pl.ds(start, length)
        return remote(
            own_rel.at[rows, pl.ds(mine, part)], xbuf.at[rows],
            x_send.at[i], x_recv.at[i], right, y,
        )

    own_loads[0].wait()

    def first_part(i, carry):
        arrange(mine, i * step)
        piece(pl.multiple_of(i * step, step), step, i).start()
        return carry

    lax.fori_loop(0, full, first_part, 0)
    arrange(mine, full * step)
    for i in range(full, len(slices)):
        piece(*slices[i], i).start()

    coul_rows = pl.ds(mine, part)
    couls = [
        send(coul.at[coul_rows], coul_left.at[coul_rows], coul_send.at[0], coul_recv.at[0], right, y),
        send(coul.at[coul_rows], coul_right.at[coul_rows], coul_send.at[1], coul_recv.at[1], left, y),
    ]

    for copy in own_loads[1:]:
        copy.wait()
    for d in range(1, times):
        base = pl.multiple_of(later[d] * part, part)

        def other_part(i, carry, base=base):
            arrange(base, i * step)
            return carry

        lax.fori_loop(0, orb // step, other_part, 0)

    def fold(lefts, column):
        span = 2 * group

        def body(i, carry):
            base = i * span
            for q in range(0, span, 2):
                x = [
                    own[base + q + k] * mask[i * (span // group) + q // group]
                    for k in range(2)
                ]
                g = mm(lefts, jnp.concatenate(x, axis=1)).astype(BF)
                for k in range(2):
                    stage[q + k] = g[:, k * orb : (k + 1) * orb]
            for b in range(0, orb, group):
                for g in range(0, span, group):
                    side[pl.ds(b, group), pl.ds(pl.multiple_of(column + base + g, group), group)] = (
                        jnp.swapaxes(stage[pl.ds(g, group), pl.ds(b, group), :], 0, 1)
                    )
            return carry

        lax.fori_loop(0, aux // span, body, 0)

    def prev_side(d, i):
        l_prev[i] = flip(occ_prev[d])
        w_prev[:, pl.ds(i * orb, orb)] = flip(virt_prev[d])
        fold(l_prev[i], 2 * i * aux)

    def edge_side(d, i):
        w_edge[:, pl.ds(i * orb, orb)] = virt_edge[d]
        fold(occ_edge[d], (2 * i + 1) * aux)

    for copy in tile_loads:
        copy.wait()
    prev_side(0, 0)

    for copy in edges:
        copy.wait_recv()
    passed = []
    for d in range(1, times):
        for k, where in enumerate((occ_edge, virt_edge)):
            passed.append(send(
                where.at[0], where.at[d], edge_send.at[d, k], edge_recv.at[d, k], me, before[d]
            ))
    edge_side(0, 0)

    for copy in tiles:
        copy.wait_recv()
    for d in range(times):
        w_own[:, pl.ds(d * orb, orb)] = flip(virt_own[d])

    some = min(part, 2 * group)

    def diagonal(i, carry):
        base = pl.multiple_of(mine + i * some, group)
        for quad in range(0, some, 4):
            held = mask[(base + quad) // group]
            x = own[pl.ds(base + quad, 4)] * held[None]
            half = mm(x.reshape(4 * orb, orb), w_own[...]).astype(BF)
            for d in range(times):
                columns = [
                    half[q * orb : (q + 1) * orb, d * orb : (d + 1) * orb] for q in range(4)
                ]
                pair = mm(occ_own[d], jnp.concatenate(columns, axis=1)).astype(BF)
                for q in range(4):
                    stage[d * some + quad + q] = pair[:, q * orb : (q + 1) * orb]
        for d in range(times):
            for b in range(0, orb, group):
                for g in range(0, some, group):
                    at = pl.multiple_of(d * part + i * some + g, group)
                    diag_rel[pl.ds(b, group), pl.ds(at, group)] = jnp.swapaxes(
                        stage[pl.ds(d * some + g, group), pl.ds(b, group), :], 0, 1
                    )
        return carry

    lax.fori_loop(0, part // some, diagonal, 0)

    acc_diag[...] = jnp.zeros_like(acc_diag)
    deep = 2 * step

    def respond_diag(i, carry):
        a = lay([diag_rel[i * deep + k] for k in range(deep)])
        b = lay([own_rel[i * deep + k] for k in range(deep)])
        acc_diag[...] += mm_nt(a, b)
        return carry

    lax.fori_loop(0, orb // deep, respond_diag, 0)
    for copy in late_loads:
        copy.wait()

    def weigh(e, read):
        total = cos[later[e], later[0]] * read(0)
        for d in range(1, times):
            total = total + cos[later[e], later[d]] * read(d)
        return total.astype(BF)

    z_copies = []
    for e in range(times):
        z_send[e, 0] = weigh(e, lambda d: acc_diag[pl.ds(d * part, part)])
        if e:
            z_copies.append(send(
                z_send.at[e, 0], z_recv.at[0, y], zs_send.at[0, e], zs_recv.at[0, e],
                me, later[e],
            ))
    z_recv[0, y] = z_send[0, 0]

    for copy in couls:
        copy.wait_recv()
    handed = []
    for d in range(1, times):
        for k, where in enumerate((coul_left, coul_right)):
            handed.append(send(
                where.at[coul_rows], where.at[coul_rows],
                pass_send.at[d, k], pass_recv.at[d, k], me, later[d],
            ))

    acc[...] = jnp.zeros_like(acc)
    for first in range(0, times, batch):
        for i in range(batch):
            d = first + i
            if d:
                if d == 1:
                    for copy in passed:
                        copy.wait_recv()
                prev_side(d, i)
                edge_side(d, i)

        def respond(start, length):
            x = xbuf[pl.ds(start, length)].reshape(length * part, orb)
            for k, weights in enumerate((w_prev, w_edge)):
                half = mm(x, weights[...]).astype(BF)
                for i in range(batch):
                    a = lay([
                        half[j * part : (j + 1) * part, i * orb : (i + 1) * orb]
                        for j in range(length)
                    ])
                    b = lay([
                        side[start + j, pl.ds((2 * i + k) * aux, aux)] for j in range(length)
                    ])
                    acc[first + i, k] += mm_nt(a, b)

        def arrived(i, carry):
            if first == 0:
                piece(pl.multiple_of(i * step, step), step, i).wait_recv()
            respond(i * step, step)
            return carry

        lax.fori_loop(0, full, arrived, 0)
        for i in range(full, len(slices)):
            if first == 0:
                piece(*slices[i], i).wait_recv()
            respond(*slices[i])

    for e in range(times):
        for k in range(2):
            z_send[e, 1 + k] = weigh(e, lambda d, k=k: acc[d, k])
        z_copies.append(send(
            z_send.at[e, 2], z_recv.at[2, y], zs_send.at[2, e], zs_recv.at[2, e],
            left, later[e],
        ))
        if e:
            z_copies.append(send(
                z_send.at[e, 1], z_recv.at[1, y], zs_send.at[1, e], zs_recv.at[1, e],
                me, later[e],
            ))
    z_recv[1, y] = z_send[0, 1]
    coul_left_own = handed
    for copy in coul_left_own + z_copies:
        copy.wait_recv()

    result = mm_tn(z_recv[0].reshape(aux, aux), coul_own[...])
    result = result + mm_tn(z_recv[1].reshape(aux, aux), coul_left[...])
    out[0] = result + mm(z_recv[2].reshape(aux, aux), coul_right[...])
    for copy in tiles + edges + passed + couls + handed + z_copies:
        copy.wait_send()
    for i in range(len(slices)):
        piece(*slices[i], i).wait_send()


def solution(mesh):
    chain, times = mesh.shape["orb"], mesh.shape["tm"]

    def body(integrals, block_map, green_occ, green_virt, coulomb, cosine):
        aux, orb = integrals.shape[0], integrals.shape[1]
        kw = coulomb.shape[1]
        part = aux // times
        group = aux // block_map.shape[0]
        step = 16
        batch = 2 - times % 2
        count = len(plan(orb, step))
        any_space = pl.BlockSpec(memory_space=pl.ANY)
        dma = pltpu.SemaphoreType.DMA
        scratch = [
            pltpu.VMEM((aux, orb, orb), BF),
            pltpu.VMEM((orb, aux, orb), BF),
            pltpu.VMEM((orb, part, orb), BF),
            pltpu.VMEM((orb, 2 * batch * aux, orb), BF),
            pltpu.VMEM((orb, aux, orb), BF),
            pltpu.VMEM((max(2 * group, times * min(part, 2 * group)), orb, orb), BF),
            pltpu.VMEM(block_map.shape[::-1], jnp.int32),
            pltpu.VMEM((block_map.shape[0], orb, orb), BF),
            pltpu.SMEM(cosine.shape, F32),
            *[pltpu.VMEM((times, orb, orb), BF)] * 6,
            pltpu.VMEM((batch, orb, orb), BF),
            pltpu.VMEM((orb, batch * orb), BF),
            pltpu.VMEM((orb, times * orb), BF),
            pltpu.VMEM((orb, batch * orb), BF),
            *[pltpu.VMEM((aux, kw), BF)] * 3,
            pltpu.VMEM((times, 2, part, aux), F32),
            pltpu.VMEM((aux, aux), F32),
            pltpu.VMEM((times, 3, part, aux), BF),
            pltpu.VMEM((3, times, part, aux), BF),
            dma((7,)), dma((times,)),
            dma((count,)), dma((count,)),
            dma((times, 2)), dma((times, 2)),
            dma((times, 4)), dma((times, 4)),
            dma((2,)), dma((2,)),
            dma((times, 2)), dma((times, 2)),
            dma((3, times)), dma((3, times)),
        ]
        return pl.pallas_call(
            functools.partial(kernel, chain, times, batch, step),
            out_shape=jax.ShapeDtypeStruct((1, aux, kw), F32),
            in_specs=[any_space] * 6,
            out_specs=pl.BlockSpec(memory_space=pltpu.VMEM),
            scratch_shapes=scratch,
            compiler_params=pltpu.CompilerParams(
                collective_id=0, has_side_effects=True, vmem_limit_bytes=56 * 2**20
            ),
        )(integrals, block_map.T, green_occ, green_virt, coulomb, cosine)

    in_specs = (
        P("orb", None, None),
        P("orb", None),
        P("tm", "orb", None),
        P("tm", "orb", None),
        P("orb", None),
        P(),
    )
    out_specs = P("tm", "orb", None)
    return jax.shard_map(body, mesh=mesh, in_specs=in_specs, out_specs=out_specs, check_vma=False)
```

```python
import functools

import jax
import jax.numpy as jnp
from jax import lax
from jax.experimental import pallas as pl
from jax.experimental.pallas import tpu as pltpu
from jax.sharding import PartitionSpec as P

MESH = pl.DeviceIdType.MESH
BF = jnp.bfloat16
F32 = jnp.float32
PAD = 4


def mm(a, b):
    return jnp.dot(a, b, preferred_element_type=F32)


def mm_nt(a, b):
    return lax.dot_general(a, b, (((1,), (1,)), ((), ())), preferred_element_type=F32)


def mm_tn(a, b):
    return lax.dot_general(a, b, (((0,), (0,)), ((), ())), preferred_element_type=F32)


def flip(tile):
    return tile.astype(F32).T.astype(BF)


def lay(parts):
    return parts[0] if len(parts) == 1 else jnp.concatenate(parts, axis=1)


def plan(orb, step):
    full = orb // step - 1
    cuts, start = [(i * step, step) for i in range(full)], full * step
    for length in (step // 2, step // 4, step // 4):
        cuts.append((start, length))
        start += length
    return cuts


def kernel(
    chain, times, batch, step,
    ints, bmap, occ, virt, coul, cosine, out,
    own, own_rel, xbuf, side, diag_rel, stage, bm, mask, cos,
    occ_prev, occ_own, occ_edge, virt_prev, virt_own, virt_edge,
    l_side, w_prev, w_own, w_edge, coul_own, coul_left,
    acc, acc_diag, z_send, z_recv, z_side, z_edge, p_send, p_recv,
    load_sem, own_sem, x_send, x_recv, edge_send, edge_recv, tile_send, tile_recv,
    coul_send, coul_recv, pass_send, pass_recv, zs_send, zs_recv,
):
    aux, orb = ints.shape[0], ints.shape[1]
    part = aux // times
    col_blocks, row_blocks = bmap.shape
    width = orb // col_blocks
    group = aux // row_blocks
    pitch = orb + PAD
    me = lax.axis_index("orb")
    y = lax.axis_index("tm")
    right = lax.rem(me + 1, chain)
    left = lax.rem(me + chain - 1, chain)
    later = [lax.rem(y + d, times) for d in range(times)]
    before = [lax.rem(y + times - d, times) for d in range(times)]

    barrier = pltpu.get_barrier_semaphore()
    for d in range(times):
        for where in (left, right) + ((me,) if d else ()):
            pl.semaphore_signal(
                barrier, inc=1, device_id=(where, later[d]), device_id_type=MESH
            )

    def load(src, dst, sem):
        copy = pltpu.make_async_copy(src, dst, sem)
        copy.start()
        return copy

    mine = pl.multiple_of(y * part, part)
    map_load = load(bmap, bm, load_sem.at[0])
    own_loads = []
    for d in range(times):
        rows = pl.ds(pl.multiple_of(later[d] * part, part), part)
        own_loads.append(load(ints.at[rows], own.at[rows], own_sem.at[d]))
    tile_loads = []
    for k, (src, prev, mid) in enumerate(
        ((occ, occ_prev, occ_own), (virt, virt_prev, virt_own))
    ):
        tile_loads.append(load(src.at[0, :, pl.ds(0, orb)], prev.at[0], load_sem.at[1 + k]))
        tile_loads.append(load(src.at[0, :, pl.ds(orb, orb)], mid.at[0], load_sem.at[3 + k]))
    late_loads = [load(coul, coul_own, load_sem.at[5]), load(cosine, cos, load_sem.at[6])]

    pl.semaphore_wait(barrier, 3 * times - 1)

    def remote(src, dst, s, r, where, peer):
        return pltpu.make_async_remote_copy(
            src_ref=src, dst_ref=dst, send_sem=s, recv_sem=r,
            device_id=(where, peer), device_id_type=MESH,
        )

    def send(*args):
        copy = remote(*args)
        copy.start()
        return copy

    edges = []
    for k, (src, dst) in enumerate(((occ, occ_edge), (virt, virt_edge))):
        edges.append(send(
            src.at[0, :, pl.ds(2 * orb, orb)], dst.at[0],
            edge_send.at[0, k], edge_recv.at[0, k], right, y,
        ))
    coul_rows = pl.ds(mine, part)
    couls = [
        send(coul.at[coul_rows], coul_left.at[coul_rows], coul_send, coul_recv, right, y),
    ]
    tiles = []
    for d in range(1, times):
        for k, (src, dst, place) in enumerate((
            (occ, occ_own, 1), (virt, virt_own, 1), (occ, occ_prev, 0), (virt, virt_prev, 0),
        )):
            tiles.append(send(
                src.at[0, :, pl.ds(place * orb, orb)], dst.at[d],
                tile_send.at[d, k], tile_recv.at[d, k], me, before[d],
            ))

    map_load.wait()
    values = bm[...].astype(F32)
    for r in range(row_blocks):
        for c in range(col_blocks):
            mask[r, pl.ds(c * width, width), :] = jnp.broadcast_to(
                values[c : c + 1, r : r + 1], (width, orb)
            ).astype(BF)

    def arrange(first, block):
        rows = pl.ds(pl.multiple_of(block, group), group)
        for g in range(part // group):
            at = pl.multiple_of(first + g * group, group)
            tile = own[pl.ds(at, group), rows, :] * mask[at // group, rows, :][None]
            own[pl.ds(at, group), rows, :] = tile
            own_rel[rows, pl.ds(at, group), :] = jnp.swapaxes(tile, 0, 1)

    slices = plan(orb, step)
    full = orb // step - 1

    def piece(start, length, i):
        rows = pl.ds(start, length)
        return remote(
            own_rel.at[rows, pl.ds(mine, part)], xbuf.at[rows],
            x_send.at[i], x_recv.at[i], right, y,
        )

    own_loads[0].wait()

    def first_part(i, carry):
        for b in range(0, step, group):
            arrange(mine, i * step + b)
        piece(pl.multiple_of(i * step, step), step, i).start()
        return carry

    lax.fori_loop(0, full, first_part, 0)
    for b in range(0, step, group):
        arrange(mine, full * step + b)
    for i in range(full, len(slices)):
        piece(*slices[i], i).start()

    for copy in own_loads[1:]:
        copy.wait()
    for d in range(1, times):
        base = pl.multiple_of(later[d] * part, part)

        def other_part(i, carry, base=base):
            arrange(base, i * group)
            return carry

        lax.fori_loop(0, orb // group, other_part, 0)

    def fold(i):
        span = 2 * group

        def body(j, carry):
            base = pl.multiple_of(j * span, span)
            for q in range(0, span, 2):
                x = jnp.concatenate([own[base + q], own[base + q + 1]], axis=1)
                g = mm(l_side[i], x)
                for k in range(2):
                    for c in range(2):
                        stage[k, pl.ds((q + c) * pitch, orb)] = g[
                            k * orb : (k + 1) * orb, c * orb : (c + 1) * orb
                        ]
            for k in range(2):
                for g in range(0, span, group):
                    at = pl.multiple_of((2 * i + k) * aux + base + g, group)
                    for m in range(orb):
                        side[m, pl.ds(at, group)] = stage[
                            k, pl.ds(g * pitch + m, group, stride=pitch), :
                        ].astype(BF)
            return carry

        lax.fori_loop(0, aux // span, body, 0)

    def sides(d, i):
        lanes = pl.ds(i * orb, orb)
        l_side[i, :orb] = flip(occ_prev[d])
        l_side[i, orb:] = occ_edge[d]
        w_prev[:, lanes] = flip(virt_prev[d])
        w_edge[:, lanes] = virt_edge[d]
        fold(i)

    for copy in tile_loads:
        copy.wait()
    for copy in edges:
        copy.wait_recv()
    passed = []
    for d in range(1, times):
        for k, where in enumerate((occ_edge, virt_edge)):
            passed.append(send(
                where.at[0], where.at[d], edge_send.at[d, k], edge_recv.at[d, k], me, before[d]
            ))
    sides(0, 0)

    for copy in tiles:
        copy.wait_recv()
    for d in range(times):
        w_own[:, pl.ds(d * orb, orb)] = flip(virt_own[d])

    some = min(part, 2 * group)

    def diagonal(i, carry):
        base = pl.multiple_of(mine + i * some, group)
        for quad in range(0, some, 4):
            x = own[pl.ds(base + quad, 4)]
            half = mm(x.reshape(4 * orb, orb), w_own[...]).astype(BF)
            for d in range(times):
                columns = [
                    half[q * orb : (q + 1) * orb, d * orb : (d + 1) * orb] for q in range(4)
                ]
                pair = mm(occ_own[d], jnp.concatenate(columns, axis=1))
                for q in range(4):
                    stage[d, pl.ds((quad + q) * pitch, orb)] = pair[:, q * orb : (q + 1) * orb]
        for d in range(times):
            for g in range(0, some, group):
                at = pl.multiple_of(d * part + i * some + g, group)
                for m in range(orb):
                    diag_rel[m, pl.ds(at, group)] = stage[
                        d, pl.ds(g * pitch + m, group, stride=pitch), :
                    ].astype(BF)
        return carry

    lax.fori_loop(0, part // some, diagonal, 0)

    acc_diag[...] = jnp.zeros_like(acc_diag)
    deep = step

    def respond_diag(i, carry):
        a = lay([diag_rel[i * deep + k] for k in range(deep)])
        b = lay([own_rel[i * deep + k] for k in range(deep)])
        acc_diag[...] += mm_nt(a, b)
        return carry

    lax.fori_loop(0, orb // deep, respond_diag, 0)
    for copy in late_loads:
        copy.wait()

    def weigh(e, read):
        total = cos[later[e], later[0]] * read(0)
        for d in range(1, times):
            total = total + cos[later[e], later[d]] * read(d)
        return total.astype(BF)

    diag_copies, z_copies = [], []
    for e in range(times):
        z_send[e] = weigh(e, lambda d: acc_diag[pl.ds(d * part, part)])
        if e:
            diag_copies.append(send(
                z_send.at[e], z_recv.at[y], zs_send.at[0, e], zs_recv.at[0, e],
                me, later[e],
            ))
    z_recv[y] = z_send[0]

    for copy in couls:
        copy.wait_recv()
    handed = []
    for d in range(1, times):
        handed.append(send(
            coul_left.at[coul_rows], coul_left.at[coul_rows],
            pass_send.at[d], pass_recv.at[d], me, later[d],
        ))

    acc[...] = jnp.zeros_like(acc)
    for first in range(0, times, batch):
        for i in range(batch):
            d = first + i
            if d:
                if d == 1:
                    for copy in passed:
                        copy.wait_recv()
                sides(d, i)

        def respond(start, length):
            x = xbuf[pl.ds(start, length)].reshape(length * part, orb)
            for k, weights in enumerate((w_prev, w_edge)):
                half = mm(x, weights[...]).astype(BF)
                for i in range(batch):
                    a = lay([
                        half[j * part : (j + 1) * part, i * orb : (i + 1) * orb]
                        for j in range(length)
                    ])
                    b = lay([
                        side[start + j, pl.ds((2 * i + k) * aux, aux)] for j in range(length)
                    ])
                    acc[first + i, k] += mm_nt(b, a)

        def arrived(i, carry):
            if first == 0:
                piece(pl.multiple_of(i * step, step), step, i).wait_recv()
            respond(i * step, step)
            return carry

        lax.fori_loop(0, full, arrived, 0)
        for i in range(full, len(slices)):
            if first == 0:
                piece(*slices[i], i).wait_recv()
            respond(*slices[i])

    for e in range(times):
        z_side[e] = weigh(e, lambda d: acc[d, 0])
        if e:
            z_copies.append(send(
                z_side.at[e], z_edge.at[y], zs_send.at[1, e], zs_recv.at[1, e],
                me, later[e],
            ))
    z_edge[y] = z_side[0]
    for e in range(times):
        panel = mm_tn(weigh(e, lambda d: acc[d, 1]), coul_own[...])
        p_send[e] = panel.astype(BF)
        z_copies.append(send(
            p_send.at[e], p_recv.at[y], zs_send.at[2, e], zs_recv.at[2, e], left, later[e],
        ))
    for copy in diag_copies:
        copy.wait_recv()
    out[0] = mm_tn(z_recv[...].reshape(aux, aux), coul_own[...])
    for copy in handed + z_copies:
        copy.wait_recv()
    edge = mm(lay([z_edge[k] for k in range(times)]), coul_left[...])
    out[0] += edge + p_recv[...].reshape(aux, out.shape[2]).astype(F32)
    for copy in tiles + edges + passed + couls + handed + diag_copies + z_copies:
        copy.wait_send()
    for i in range(len(slices)):
        piece(*slices[i], i).wait_send()


def solution(mesh):
    chain, times = mesh.shape["orb"], mesh.shape["tm"]

    def body(integrals, block_map, green_occ, green_virt, coulomb, cosine):
        aux, orb = integrals.shape[0], integrals.shape[1]
        kw = coulomb.shape[1]
        part = aux // times
        group = aux // block_map.shape[0]
        step = orb // 4
        batch = 2 - times % 2
        count = len(plan(orb, step))
        any_space = pl.BlockSpec(memory_space=pl.ANY)
        dma = pltpu.SemaphoreType.DMA
        scratch = [
            pltpu.VMEM((aux, orb, orb), BF),
            pltpu.VMEM((orb, aux, orb), BF),
            pltpu.VMEM((orb, part, orb), BF),
            pltpu.VMEM((orb, 2 * batch * aux, orb), BF),
            pltpu.VMEM((orb, aux, orb), BF),
            pltpu.VMEM((max(2, times), 2 * group * (orb + PAD), orb), F32),
            pltpu.VMEM(block_map.shape[::-1], jnp.int32),
            pltpu.VMEM((block_map.shape[0], orb, orb), BF),
            pltpu.SMEM(cosine.shape, F32),
            *[pltpu.VMEM((times, orb, orb), BF)] * 6,
            pltpu.VMEM((batch, 2 * orb, orb), BF),
            pltpu.VMEM((orb, batch * orb), BF),
            pltpu.VMEM((orb, times * orb), BF),
            pltpu.VMEM((orb, batch * orb), BF),
            *[pltpu.VMEM((aux, kw), BF)] * 2,
            pltpu.VMEM((times, 2, aux, part), F32),
            pltpu.VMEM((aux, aux), F32),
            pltpu.VMEM((times, part, aux), BF),
            pltpu.VMEM((times, part, aux), BF),
            *[pltpu.VMEM((times, aux, part), BF)] * 2,
            *[pltpu.VMEM((times, part, kw), BF)] * 2,
            dma((7,)), dma((times,)),
            dma((count,)), dma((count,)),
            dma((times, 2)), dma((times, 2)),
            dma((times, 4)), dma((times, 4)),
            dma, dma,
            dma((times,)), dma((times,)),
            dma((3, times)), dma((3, times)),
        ]
        return pl.pallas_call(
            functools.partial(kernel, chain, times, batch, step),
            out_shape=jax.ShapeDtypeStruct((1, aux, kw), F32),
            in_specs=[any_space] * 6,
            out_specs=pl.BlockSpec(memory_space=pltpu.VMEM),
            scratch_shapes=scratch,
            compiler_params=pltpu.CompilerParams(
                collective_id=0, has_side_effects=True, vmem_limit_bytes=56 * 2**20
            ),
        )(integrals, block_map.T, green_occ, green_virt, coulomb, cosine)

    in_specs = (
        P("orb", None, None),
        P("orb", None),
        P("tm", "orb", None),
        P("tm", "orb", None),
        P("orb", None),
        P(),
    )
    out_specs = P("tm", "orb", None)
    return jax.shard_map(body, mesh=mesh, in_specs=in_specs, out_specs=out_specs, check_vma=False)
```

```python
import functools

import jax
import jax.numpy as jnp
from jax import lax
from jax.experimental import pallas as pl
from jax.experimental.pallas import tpu as pltpu
from jax.sharding import PartitionSpec as P

MESH = pl.DeviceIdType.MESH
BF = jnp.bfloat16
F32 = jnp.float32
PAD = 4


def mm(a, b):
    return jnp.dot(a, b, preferred_element_type=F32)


def mm_nt(a, b):
    return lax.dot_general(a, b, (((1,), (1,)), ((), ())), preferred_element_type=F32)


def mm_tn(a, b):
    return lax.dot_general(a, b, (((0,), (0,)), ((), ())), preferred_element_type=F32)


def flip(tile):
    return tile.astype(F32).T.astype(BF)


def lay(parts):
    return parts[0] if len(parts) == 1 else jnp.concatenate(parts, axis=1)


def plan(orb, step):
    full = orb // step - 1
    cuts, start = [(i * step, step) for i in range(full)], full * step
    for length in (step // 2, step // 4, step // 4):
        cuts.append((start, length))
        start += length
    return cuts


def kernel(
    chain, times, batch, step,
    ints, bmap, occ, virt, coul, cosine, out,
    own, own_rel, xbuf, side, diag_rel, stage, bm, mask, cos,
    occ_prev, occ_own, occ_edge, virt_prev, virt_own, virt_edge,
    l_side, w_prev, w_own, w_edge, coul_own, coul_left,
    acc, acc_diag, z_send, z_recv, z_side, z_edge, p_send, p_recv,
    load_sem, first_sem, own_sem, x_send, x_recv, edge_send, edge_recv, tile_send, tile_recv,
    coul_send, coul_recv, zs_send, zs_recv, hello,
):
    aux, orb = ints.shape[0], ints.shape[1]
    part = aux // times
    col_blocks, row_blocks = bmap.shape
    width = orb // col_blocks
    group = aux // row_blocks
    pitch = orb + PAD
    me = lax.axis_index("orb")
    y = lax.axis_index("tm")
    right = lax.rem(me + 1, chain)
    left = lax.rem(me + chain - 1, chain)
    later = [lax.rem(y + d, times) for d in range(times)]
    before = [lax.rem(y + times - d, times) for d in range(times)]

    barrier = pltpu.get_barrier_semaphore()
    def load(src, dst, sem):
        copy = pltpu.make_async_copy(src, dst, sem)
        copy.start()
        return copy

    mine = pl.multiple_of(y * part, part)
    map_load = load(bmap, bm, load_sem.at[0])
    first_loads = []
    for i in range(orb // step):
        at = (pl.ds(mine, part), pl.ds(i * step, step))
        first_loads.append(load(ints.at[at], own.at[at], first_sem.at[i]))
    pl.semaphore_signal(barrier, inc=1, device_id=(left, y), device_id_type=MESH)
    for d in range(1, times):
        @pl.when(y + d < times)
        def _(d=d):
            pl.semaphore_signal(barrier, inc=1, device_id=(me, later[d]), device_id_type=MESH)

    own_loads = []
    for d in range(1, times):
        rows = pl.ds(pl.multiple_of(later[d] * part, part), part)
        own_loads.append(load(ints.at[rows], own.at[rows], own_sem.at[d]))
    tile_loads = []
    for k, (src, prev, mid) in enumerate(
        ((occ, occ_prev, occ_own), (virt, virt_prev, virt_own))
    ):
        tile_loads.append(load(src.at[0, :, pl.ds(0, orb)], prev.at[0], load_sem.at[1 + k]))
        tile_loads.append(load(src.at[0, :, pl.ds(orb, orb)], mid.at[0], load_sem.at[3 + k]))
    late_loads = [load(coul, coul_own, load_sem.at[5]), load(cosine, cos, load_sem.at[6])]

    pl.semaphore_wait(barrier, 1 + y)
    for d in range(1, times):
        @pl.when(y >= d)
        def _(d=d):
            pl.semaphore_signal(hello.at[d], inc=1, device_id=(me, before[d]), device_id_type=MESH)

    def remote(src, dst, s, r, where, peer):
        return pltpu.make_async_remote_copy(
            src_ref=src, dst_ref=dst, send_sem=s, recv_sem=r,
            device_id=(where, peer), device_id_type=MESH,
        )

    def send(*args):
        copy = remote(*args)
        copy.start()
        return copy

    edges = []
    for k, (src, dst) in enumerate(((occ, occ_edge), (virt, virt_edge))):
        edges.append(send(
            src.at[0, :, pl.ds(2 * orb, orb)], dst.at[0],
            edge_send.at[0, k], edge_recv.at[0, k], right, y,
        ))
    tiles = [[] for _ in range(times)]
    for d in range(1, times):
        for k, (src, dst, place) in enumerate((
            (occ, occ_own, 1), (virt, virt_own, 1), (occ, occ_prev, 0), (virt, virt_prev, 0),
        )):
            tiles[d].append(remote(
                src.at[0, :, pl.ds(place * orb, orb)], dst.at[d],
                tile_send.at[d, k], tile_recv.at[d, k], me, before[d],
            ))

        @pl.when(y >= d)
        def _(d=d):
            for copy in tiles[d]:
                copy.start()

    map_load.wait()
    values = bm[...].astype(F32)
    for r in range(row_blocks):
        for c in range(col_blocks):
            mask[r, pl.ds(c * width, width), :] = jnp.broadcast_to(
                values[c : c + 1, r : r + 1], (width, orb)
            ).astype(BF)

    def arrange(first, block):
        rows = pl.ds(pl.multiple_of(block, group), group)
        for g in range(part // group):
            at = pl.multiple_of(first + g * group, group)
            tile = own[pl.ds(at, group), rows, :] * mask[at // group, rows, :][None]
            own[pl.ds(at, group), rows, :] = tile
            own_rel[rows, pl.ds(at, group), :] = jnp.swapaxes(tile, 0, 1)

    slices = plan(orb, step)
    full = orb // step - 1

    def piece(start, length, i):
        rows = pl.ds(start, length)
        return remote(
            own_rel.at[rows, pl.ds(mine, part)], xbuf.at[rows],
            x_send.at[i], x_recv.at[i], right, y,
        )

    def first_part(i, carry):
        at = (pl.ds(mine, part), pl.ds(pl.multiple_of(i * step, step), step))
        pltpu.make_async_copy(ints.at[at], own.at[at], first_sem.at[i]).wait()
        for b in range(0, step, group):
            arrange(mine, i * step + b)
        piece(pl.multiple_of(i * step, step), step, i).start()
        return carry

    lax.fori_loop(0, full, first_part, 0)
    first_loads[full].wait()
    for b in range(0, step, group):
        arrange(mine, full * step + b)
    for i in range(full, len(slices)):
        piece(*slices[i], i).start()
    for d in range(1, times):
        @pl.when(y < d)
        def _(d=d):
            pl.semaphore_wait(hello.at[times - d], 1)
            for copy in tiles[d]:
                copy.start()

    tiles = [copy for row in tiles for copy in row]
    couls = [send(coul, coul_left, coul_send, coul_recv, right, y)]

    for copy in own_loads:
        copy.wait()
    for d in range(1, times):
        base = pl.multiple_of(later[d] * part, part)

        def other_part(i, carry, base=base):
            arrange(base, i * group)
            return carry

        lax.fori_loop(0, orb // group, other_part, 0)

    def fold(i):
        span = 2 * group

        def body(j, carry):
            base = pl.multiple_of(j * span, span)
            for q in range(0, span, 2):
                x = jnp.concatenate([own[base + q], own[base + q + 1]], axis=1)
                g = mm(l_side[i], x)
                for k in range(2):
                    for c in range(2):
                        stage[k, pl.ds((q + c) * pitch, orb)] = g[
                            k * orb : (k + 1) * orb, c * orb : (c + 1) * orb
                        ]
            for k in range(2):
                for g in range(0, span, group):
                    at = pl.multiple_of((2 * i + k) * aux + base + g, group)
                    for m in range(orb):
                        side[m, pl.ds(at, group)] = stage[
                            k, pl.ds(g * pitch + m, group, stride=pitch), :
                        ].astype(BF)
            return carry

        lax.fori_loop(0, aux // span, body, 0)

    def sides(d, i):
        lanes = pl.ds(i * orb, orb)
        l_side[i, :orb] = flip(occ_prev[d])
        l_side[i, orb:] = occ_edge[d]
        w_prev[:, lanes] = flip(virt_prev[d])
        w_edge[:, lanes] = virt_edge[d]
        fold(i)

    for copy in tile_loads:
        copy.wait()
    for copy in edges:
        copy.wait_recv()
    passed = []
    for d in range(1, times):
        for k, where in enumerate((occ_edge, virt_edge)):
            passed.append(send(
                where.at[0], where.at[d], edge_send.at[d, k], edge_recv.at[d, k], me, before[d]
            ))
    sides(0, 0)

    for copy in tiles:
        copy.wait_recv()
    for d in range(times):
        w_own[:, pl.ds(d * orb, orb)] = flip(virt_own[d])

    some = min(part, 2 * group)

    def diagonal(i, carry):
        base = pl.multiple_of(mine + i * some, group)
        for quad in range(0, some, 4):
            x = own[pl.ds(base + quad, 4)]
            half = mm(x.reshape(4 * orb, orb), w_own[...]).astype(BF)
            for d in range(times):
                columns = [
                    half[q * orb : (q + 1) * orb, d * orb : (d + 1) * orb] for q in range(4)
                ]
                pair = mm(occ_own[d], jnp.concatenate(columns, axis=1))
                for q in range(4):
                    stage[d, pl.ds((quad + q) * pitch, orb)] = pair[:, q * orb : (q + 1) * orb]
        for d in range(times):
            for g in range(0, some, group):
                at = pl.multiple_of(d * part + i * some + g, group)
                for m in range(orb):
                    diag_rel[m, pl.ds(at, group)] = stage[
                        d, pl.ds(g * pitch + m, group, stride=pitch), :
                    ].astype(BF)
        return carry

    lax.fori_loop(0, part // some, diagonal, 0)

    acc_diag[...] = jnp.zeros_like(acc_diag)
    deep = step

    def respond_diag(i, carry):
        a = lay([diag_rel[i * deep + k] for k in range(deep)])
        b = lay([own_rel[i * deep + k] for k in range(deep)])
        acc_diag[...] += mm_nt(a, b)
        return carry

    lax.fori_loop(0, orb // deep, respond_diag, 0)
    for copy in late_loads:
        copy.wait()

    def weigh(e, read):
        total = cos[later[e], later[0]] * read(0)
        for d in range(1, times):
            total = total + cos[later[e], later[d]] * read(d)
        return total.astype(BF)

    diag_copies, z_copies = [], []
    for e in range(times):
        z_send[e] = weigh(e, lambda d: acc_diag[pl.ds(d * part, part)])
        if e:
            diag_copies.append(send(
                z_send.at[e], z_recv.at[y], zs_send.at[0, e], zs_recv.at[0, e],
                me, later[e],
            ))
    z_recv[y] = z_send[0]

    acc[...] = jnp.zeros_like(acc)
    for first in range(0, times, batch):
        for i in range(batch):
            d = first + i
            if d:
                if d == 1:
                    for copy in passed:
                        copy.wait_recv()
                sides(d, i)

        def respond(start, length):
            x = xbuf[pl.ds(start, length)].reshape(length * part, orb)
            for k, weights in enumerate((w_prev, w_edge)):
                half = mm(x, weights[...]).astype(BF)
                for i in range(batch):
                    a = lay([
                        half[j * part : (j + 1) * part, i * orb : (i + 1) * orb]
                        for j in range(length)
                    ])
                    b = lay([
                        side[start + j, pl.ds((2 * i + k) * aux, aux)] for j in range(length)
                    ])
                    acc[first + i, k] += mm_nt(b, a)

        def arrived(i, carry):
            if first == 0:
                piece(pl.multiple_of(i * step, step), step, i).wait_recv()
            respond(i * step, step)
            return carry

        lax.fori_loop(0, full, arrived, 0)
        for i in range(full, len(slices)):
            if first == 0:
                piece(*slices[i], i).wait_recv()
            respond(*slices[i])

    for e in range(times):
        z_side[e] = weigh(e, lambda d: acc[d, 0])
        if e:
            z_copies.append(send(
                z_side.at[e], z_edge.at[y], zs_send.at[1, e], zs_recv.at[1, e],
                me, later[e],
            ))
    z_edge[y] = z_side[0]
    for copy in diag_copies:
        copy.wait_recv()
    for e in range(times):
        panel = mm_tn(weigh(e, lambda d: acc[d, 1]), coul_own[...])
        p_send[e] = panel.astype(BF)
        z_copies.append(send(
            p_send.at[e], p_recv.at[y], zs_send.at[2, e], zs_recv.at[2, e], left, later[e],
        ))
    out[0] = mm_tn(z_recv[...].reshape(aux, aux), coul_own[...])
    for copy in couls + z_copies:
        copy.wait_recv()
    edge = mm(lay([z_edge[k] for k in range(times)]), coul_left[...])
    out[0] += edge + p_recv[...].reshape(aux, out.shape[2]).astype(F32)
    for copy in tiles + edges + passed + couls + diag_copies + z_copies:
        copy.wait_send()
    for i in range(len(slices)):
        piece(*slices[i], i).wait_send()


def solution(mesh):
    chain, times = mesh.shape["orb"], mesh.shape["tm"]

    def body(integrals, block_map, green_occ, green_virt, coulomb, cosine):
        aux, orb = integrals.shape[0], integrals.shape[1]
        kw = coulomb.shape[1]
        part = aux // times
        group = aux // block_map.shape[0]
        step = orb // 4
        batch = 2 - times % 2
        count = len(plan(orb, step))
        any_space = pl.BlockSpec(memory_space=pl.ANY)
        dma = pltpu.SemaphoreType.DMA
        scratch = [
            pltpu.VMEM((aux, orb, orb), BF),
            pltpu.VMEM((orb, aux, orb), BF),
            pltpu.VMEM((orb, part, orb), BF),
            pltpu.VMEM((orb, 2 * batch * aux, orb), BF),
            pltpu.VMEM((orb, aux, orb), BF),
            pltpu.VMEM((max(2, times), 2 * group * (orb + PAD), orb), F32),
            pltpu.VMEM(block_map.shape[::-1], jnp.int32),
            pltpu.VMEM((block_map.shape[0], orb, orb), BF),
            pltpu.SMEM(cosine.shape, F32),
            *[pltpu.VMEM((times, orb, orb), BF)] * 6,
            pltpu.VMEM((batch, 2 * orb, orb), BF),
            pltpu.VMEM((orb, batch * orb), BF),
            pltpu.VMEM((orb, times * orb), BF),
            pltpu.VMEM((orb, batch * orb), BF),
            *[pltpu.VMEM((aux, kw), BF)] * 2,
            pltpu.VMEM((times, 2, aux, part), F32),
            pltpu.VMEM((aux, aux), F32),
            pltpu.VMEM((times, part, aux), BF),
            pltpu.VMEM((times, part, aux), BF),
            *[pltpu.VMEM((times, aux, part), BF)] * 2,
            *[pltpu.VMEM((times, part, kw), BF)] * 2,
            dma((7,)), dma((orb // step,)), dma((times,)),
            dma((count,)), dma((count,)),
            dma((times, 2)), dma((times, 2)),
            dma((times, 4)), dma((times, 4)),
            dma, dma,
            dma((3, times)), dma((3, times)),
            pltpu.SemaphoreType.REGULAR((times,)),
        ]
        return pl.pallas_call(
            functools.partial(kernel, chain, times, batch, step),
            out_shape=jax.ShapeDtypeStruct((1, aux, kw), F32),
            in_specs=[any_space] * 6,
            out_specs=pl.BlockSpec(memory_space=pltpu.VMEM),
            scratch_shapes=scratch,
            compiler_params=pltpu.CompilerParams(
                collective_id=0, has_side_effects=True, vmem_limit_bytes=56 * 2**20
            ),
        )(integrals, block_map.T, green_occ, green_virt, coulomb, cosine)

    in_specs = (
        P("orb", None, None),
        P("orb", None),
        P("tm", "orb", None),
        P("tm", "orb", None),
        P("orb", None),
        P(),
    )
    out_specs = P("tm", "orb", None)
    return jax.shard_map(body, mesh=mesh, in_specs=in_specs, out_specs=out_specs, check_vma=False)
```

```python
import functools

import jax
import jax.numpy as jnp
from jax import lax
from jax.experimental import pallas as pl
from jax.experimental.pallas import tpu as pltpu
from jax.sharding import PartitionSpec as P

MESH = pl.DeviceIdType.MESH
BF = jnp.bfloat16
F32 = jnp.float32
PAD = 4


def mm(a, b):
    return jnp.dot(a, b, preferred_element_type=F32)


def mm_nt(a, b):
    return lax.dot_general(a, b, (((1,), (1,)), ((), ())), preferred_element_type=F32)


def mm_tn(a, b):
    return lax.dot_general(a, b, (((0,), (0,)), ((), ())), preferred_element_type=F32)


def flip(tile):
    return tile.astype(F32).T.astype(BF)


def lay(parts):
    return parts[0] if len(parts) == 1 else jnp.concatenate(parts, axis=1)


def plan(orb, step):
    full = orb // step - 1
    cuts, start = [(i * step, step) for i in range(full)], full * step
    for length in (step // 2, step // 4, step // 8, step // 8):
        cuts.append((start, length))
        start += length
    return cuts


def kernel(
    chain, times, batch, step,
    ints, bmap, occ, virt, coul, cosine, out,
    own, own_rel, xbuf, side, diag_rel, stage, bm, mask, cos,
    occ_prev, occ_own, occ_edge, virt_prev, virt_own, virt_edge,
    l_side, w_prev, w_own, w_edge, coul_own, coul_left,
    acc, acc_diag, z_send, z_recv, z_side, z_edge, p_send, p_recv,
    load_sem, first_sem, own_sem, x_send, x_recv, edge_send, edge_recv, tile_send, tile_recv,
    coul_send, coul_recv, zs_send, zs_recv, hello,
):
    aux, orb = ints.shape[0], ints.shape[1]
    part = aux // times
    col_blocks, row_blocks = bmap.shape
    width = orb // col_blocks
    group = aux // row_blocks
    pitch = orb + PAD
    me = lax.axis_index("orb")
    y = lax.axis_index("tm")
    right = lax.rem(me + 1, chain)
    left = lax.rem(me + chain - 1, chain)
    later = [lax.rem(y + d, times) for d in range(times)]
    before = [lax.rem(y + times - d, times) for d in range(times)]

    barrier = pltpu.get_barrier_semaphore()
    def load(src, dst, sem):
        copy = pltpu.make_async_copy(src, dst, sem)
        copy.start()
        return copy

    mine = pl.multiple_of(y * part, part)
    map_load = load(bmap, bm, load_sem.at[0])
    first_loads = []
    for i in range(orb // step):
        at = (pl.ds(mine, part), pl.ds(i * step, step))
        first_loads.append(load(ints.at[at], own.at[at], first_sem.at[i]))
    pl.semaphore_signal(barrier, inc=1, device_id=(left, y), device_id_type=MESH)
    for d in range(1, times):
        @pl.when(y + d < times)
        def _(d=d):
            pl.semaphore_signal(barrier, inc=1, device_id=(me, later[d]), device_id_type=MESH)

    own_loads = []
    for d in range(1, times):
        rows = pl.ds(pl.multiple_of(later[d] * part, part), part)
        own_loads.append(load(ints.at[rows], own.at[rows], own_sem.at[d]))
    tile_loads = []
    for k, (src, prev, mid) in enumerate(
        ((occ, occ_prev, occ_own), (virt, virt_prev, virt_own))
    ):
        tile_loads.append(load(src.at[0, :, pl.ds(0, orb)], prev.at[0], load_sem.at[1 + k]))
        tile_loads.append(load(src.at[0, :, pl.ds(orb, orb)], mid.at[0], load_sem.at[3 + k]))
    late_loads = [load(coul, coul_own, load_sem.at[5]), load(cosine, cos, load_sem.at[6])]

    pl.semaphore_wait(barrier, 1 + y)
    for d in range(1, times):
        @pl.when(y >= d)
        def _(d=d):
            pl.semaphore_signal(hello.at[d], inc=1, device_id=(me, before[d]), device_id_type=MESH)

    def remote(src, dst, s, r, where, peer):
        return pltpu.make_async_remote_copy(
            src_ref=src, dst_ref=dst, send_sem=s, recv_sem=r,
            device_id=(where, peer), device_id_type=MESH,
        )

    def send(*args):
        copy = remote(*args)
        copy.start()
        return copy

    edges = []
    for k, (src, dst) in enumerate(((occ, occ_edge), (virt, virt_edge))):
        edges.append(send(
            src.at[0, :, pl.ds(2 * orb, orb)], dst.at[0],
            edge_send.at[0, k], edge_recv.at[0, k], right, y,
        ))
    tiles = [[] for _ in range(times)]
    for d in range(1, times):
        for k, (src, dst, place) in enumerate((
            (occ, occ_own, 1), (virt, virt_own, 1), (occ, occ_prev, 0), (virt, virt_prev, 0),
        )):
            tiles[d].append(remote(
                src.at[0, :, pl.ds(place * orb, orb)], dst.at[d],
                tile_send.at[d, k], tile_recv.at[d, k], me, before[d],
            ))

        @pl.when(y >= d)
        def _(d=d):
            for copy in tiles[d]:
                copy.start()

    map_load.wait()
    values = bm[...].astype(F32)
    for r in range(row_blocks):
        for c in range(col_blocks):
            mask[r, pl.ds(c * width, width), :] = jnp.broadcast_to(
                values[c : c + 1, r : r + 1], (width, orb)
            ).astype(BF)

    def arrange(first, block):
        rows = pl.ds(pl.multiple_of(block, group), group)
        for g in range(part // group):
            at = pl.multiple_of(first + g * group, group)
            tile = own[pl.ds(at, group), rows, :] * mask[at // group, rows, :][None]
            own[pl.ds(at, group), rows, :] = tile
            own_rel[rows, pl.ds(at, group), :] = jnp.swapaxes(tile, 0, 1)

    slices = plan(orb, step)
    full = orb // step - 1

    def piece(start, length, i):
        rows = pl.ds(start, length)
        return remote(
            own_rel.at[rows, pl.ds(mine, part)], xbuf.at[rows],
            x_send.at[i], x_recv.at[i], right, y,
        )

    def first_part(i, carry):
        at = (pl.ds(mine, part), pl.ds(pl.multiple_of(i * step, step), step))
        pltpu.make_async_copy(ints.at[at], own.at[at], first_sem.at[i]).wait()
        for b in range(0, step, group):
            arrange(mine, i * step + b)
        piece(pl.multiple_of(i * step, step), step, i).start()
        return carry

    lax.fori_loop(0, full, first_part, 0)
    first_loads[full].wait()
    for b in range(0, step, group):
        arrange(mine, full * step + b)
    ends = len(slices) - 1
    keeps = jnp.logical_or(me < chain - 1, y == 0)
    lends = jnp.logical_and(me == chain - 1, y + 1 < times)
    last = pl.ds(*slices[ends])
    next_rows = pl.ds(pl.multiple_of(later[1 % times] * part, part), part)
    lent = remote(
        own_rel.at[last, next_rows], xbuf.at[last],
        x_send.at[ends + 1], x_recv.at[ends], right, later[1 % times],
    )
    for d in range(1, times):
        @pl.when(y < d)
        def _(d=d):
            pl.semaphore_wait(hello.at[times - d], 1)
            for copy in tiles[d]:
                copy.start()

    tiles = [copy for row in tiles for copy in row]
    for copy in own_loads:
        copy.wait()
    for d in range(1, times):
        base = pl.multiple_of(later[d] * part, part)

        def other_part(i, carry, base=base):
            arrange(base, i * group)
            return carry

        lax.fori_loop(0, orb // group, other_part, 0)

    @pl.when(lends)
    def _():
        lent.start()

    for i in range(full, ends):
        piece(*slices[i], i).start()

    @pl.when(keeps)
    def _():
        piece(*slices[ends], ends).start()

    couls = [send(coul, coul_left, coul_send, coul_recv, right, y)]

    def fold(i):
        span = 2 * group

        def body(j, carry):
            base = pl.multiple_of(j * span, span)
            for q in range(0, span, 2):
                x = jnp.concatenate([own[base + q], own[base + q + 1]], axis=1)
                g = mm(l_side[i], x)
                for k in range(2):
                    for c in range(2):
                        stage[k, pl.ds((q + c) * pitch, orb)] = g[
                            k * orb : (k + 1) * orb, c * orb : (c + 1) * orb
                        ]
            for k in range(2):
                for g in range(0, span, group):
                    at = pl.multiple_of((2 * i + k) * aux + base + g, group)
                    for m in range(orb):
                        side[m, pl.ds(at, group)] = stage[
                            k, pl.ds(g * pitch + m, group, stride=pitch), :
                        ].astype(BF)
            return carry

        lax.fori_loop(0, aux // span, body, 0)

    def sides(d, i):
        lanes = pl.ds(i * orb, orb)
        l_side[i, :orb] = flip(occ_prev[d])
        l_side[i, orb:] = occ_edge[d]
        w_prev[:, lanes] = flip(virt_prev[d])
        w_edge[:, lanes] = virt_edge[d]
        fold(i)

    for copy in tile_loads:
        copy.wait()
    for copy in edges:
        copy.wait_recv()
    passed = []
    for d in range(1, times):
        for k, where in enumerate((occ_edge, virt_edge)):
            passed.append(send(
                where.at[0], where.at[d], edge_send.at[d, k], edge_recv.at[d, k], me, before[d]
            ))
    sides(0, 0)

    for copy in tiles:
        copy.wait_recv()
    for d in range(times):
        w_own[:, pl.ds(d * orb, orb)] = flip(virt_own[d])

    some = min(part, 2 * group)

    def diagonal(i, carry):
        base = pl.multiple_of(mine + i * some, group)
        for quad in range(0, some, 4):
            x = own[pl.ds(base + quad, 4)]
            half = mm(x.reshape(4 * orb, orb), w_own[...]).astype(BF)
            for d in range(times):
                columns = [
                    half[q * orb : (q + 1) * orb, d * orb : (d + 1) * orb] for q in range(4)
                ]
                pair = mm(occ_own[d], jnp.concatenate(columns, axis=1))
                for q in range(4):
                    stage[d, pl.ds((quad + q) * pitch, orb)] = pair[:, q * orb : (q + 1) * orb]
        for d in range(times):
            for g in range(0, some, group):
                at = pl.multiple_of(d * part + i * some + g, group)
                for m in range(orb):
                    diag_rel[m, pl.ds(at, group)] = stage[
                        d, pl.ds(g * pitch + m, group, stride=pitch), :
                    ].astype(BF)
        return carry

    lax.fori_loop(0, part // some, diagonal, 0)

    acc_diag[...] = jnp.zeros_like(acc_diag)
    deep = step

    def respond_diag(i, carry):
        a = lay([diag_rel[i * deep + k] for k in range(deep)])
        b = lay([own_rel[i * deep + k] for k in range(deep)])
        acc_diag[...] += mm_nt(a, b)
        return carry

    lax.fori_loop(0, orb // deep, respond_diag, 0)
    for copy in late_loads:
        copy.wait()

    def weigh(e, read):
        total = cos[later[e], later[0]] * read(0)
        for d in range(1, times):
            total = total + cos[later[e], later[d]] * read(d)
        return total.astype(BF)

    diag_copies, z_copies, p_copies = [], [], []
    for e in range(times):
        z_send[e] = weigh(e, lambda d: acc_diag[pl.ds(d * part, part)])
        if e:
            diag_copies.append(send(
                z_send.at[e], z_recv.at[y], zs_send.at[0, e], zs_recv.at[0, e],
                me, later[e],
            ))
    z_recv[y] = z_send[0]

    acc[...] = jnp.zeros_like(acc)
    for first in range(0, times, batch):
        for i in range(batch):
            d = first + i
            if d:
                if d == 1:
                    for copy in passed:
                        copy.wait_recv()
                sides(d, i)

        def respond(start, length, kinds=(0, 1)):
            x = xbuf[pl.ds(start, length)].reshape(length * part, orb)
            for k in kinds:
                weights = (w_prev, w_edge)[k]
                half = mm(x, weights[...]).astype(BF)
                for i in range(batch):
                    a = lay([
                        half[j * part : (j + 1) * part, i * orb : (i + 1) * orb]
                        for j in range(length)
                    ])
                    b = lay([
                        side[start + j, pl.ds((2 * i + k) * aux, aux)] for j in range(length)
                    ])
                    acc[first + i, k] += mm_nt(a, b)

        def arrived(i, carry):
            if first == 0:
                piece(pl.multiple_of(i * step, step), step, i).wait_recv()
            respond(i * step, step)
            return carry

        lax.fori_loop(0, full, arrived, 0)
        for i in range(full, len(slices)):
            if first == 0:
                piece(*slices[i], i).wait_recv()
            closing = i == len(slices) - 1 and first + batch == times
            respond(*slices[i], kinds=(0,) if closing else (0, 1))

    for e in (*range(1, times), 0):
        z_side[e] = weigh(e, lambda d: acc[d, 0])
        if e:
            z_copies.append(send(
                z_side.at[e], z_edge.at[y], zs_send.at[1, e], zs_recv.at[1, e],
                me, later[e],
            ))
    respond(*slices[-1], kinds=(1,))
    for copy in diag_copies:
        copy.wait_recv()
    for e in range(times):
        panel = mm(weigh(e, lambda d: acc[d, 1]), coul_own[...])
        p_send[e] = panel.astype(BF)
        p_copies.append(send(
            p_send.at[e], p_recv.at[y], zs_send.at[2, e], zs_recv.at[2, e], left, later[e],
        ))
    out[0] = mm_tn(z_recv[...].reshape(aux, aux), coul_own[...])
    z_edge[y] = z_side[0]
    for copy in couls + z_copies + p_copies:
        copy.wait_recv()
    edge = mm_tn(z_edge[...].reshape(aux, aux), coul_left[...])
    out[0] += edge + p_recv[...].reshape(aux, out.shape[2]).astype(F32)
    for copy in tiles + edges + passed + couls + diag_copies + z_copies + p_copies:
        copy.wait_send()
    for i in range(ends):
        piece(*slices[i], i).wait_send()

    @pl.when(keeps)
    def _():
        piece(*slices[ends], ends).wait_send()

    @pl.when(lends)
    def _():
        lent.wait_send()


def solution(mesh):
    chain, times = mesh.shape["orb"], mesh.shape["tm"]

    def body(integrals, block_map, green_occ, green_virt, coulomb, cosine):
        aux, orb = integrals.shape[0], integrals.shape[1]
        kw = coulomb.shape[1]
        part = aux // times
        group = aux // block_map.shape[0]
        step = orb // 4
        batch = 2 - times % 2
        count = len(plan(orb, step))
        any_space = pl.BlockSpec(memory_space=pl.ANY)
        dma = pltpu.SemaphoreType.DMA
        scratch = [
            pltpu.VMEM((aux, orb, orb), BF),
            pltpu.VMEM((orb, aux, orb), BF),
            pltpu.VMEM((orb, part, orb), BF),
            pltpu.VMEM((orb, 2 * batch * aux, orb), BF),
            pltpu.VMEM((orb, aux, orb), BF),
            pltpu.VMEM((max(2, times), 2 * group * (orb + PAD), orb), F32),
            pltpu.VMEM(block_map.shape[::-1], jnp.int32),
            pltpu.VMEM((block_map.shape[0], orb, orb), BF),
            pltpu.SMEM(cosine.shape, F32),
            *[pltpu.VMEM((times, orb, orb), BF)] * 6,
            pltpu.VMEM((batch, 2 * orb, orb), BF),
            pltpu.VMEM((orb, batch * orb), BF),
            pltpu.VMEM((orb, times * orb), BF),
            pltpu.VMEM((orb, batch * orb), BF),
            *[pltpu.VMEM((aux, kw), BF)] * 2,
            pltpu.VMEM((times, 2, part, aux), F32),
            pltpu.VMEM((aux, aux), F32),
            pltpu.VMEM((times, part, aux), BF),
            pltpu.VMEM((times, part, aux), BF),
            *[pltpu.VMEM((times, part, aux), BF)] * 2,
            *[pltpu.VMEM((times, part, kw), BF)] * 2,
            dma((7,)), dma((orb // step,)), dma((times,)),
            dma((count + 1,)), dma((count,)),
            dma((times, 2)), dma((times, 2)),
            dma((times, 4)), dma((times, 4)),
            dma, dma,
            dma((3, times)), dma((3, times)),
            pltpu.SemaphoreType.REGULAR((times,)),
        ]
        return pl.pallas_call(
            functools.partial(kernel, chain, times, batch, step),
            out_shape=jax.ShapeDtypeStruct((1, aux, kw), F32),
            in_specs=[any_space] * 6,
            out_specs=pl.BlockSpec(memory_space=pltpu.VMEM),
            scratch_shapes=scratch,
            compiler_params=pltpu.CompilerParams(
                collective_id=0, has_side_effects=True, vmem_limit_bytes=56 * 2**20
            ),
        )(integrals, block_map.T, green_occ, green_virt, coulomb, cosine)

    in_specs = (
        P("orb", None, None),
        P("orb", None),
        P("tm", "orb", None),
        P("tm", "orb", None),
        P("orb", None),
        P(),
    )
    out_specs = P("tm", "orb", None)
    return jax.shard_map(body, mesh=mesh, in_specs=in_specs, out_specs=out_specs, check_vma=False)
```

```python
import functools

import jax
import jax.numpy as jnp
from jax import lax
from jax.experimental import pallas as pl
from jax.experimental.pallas import tpu as pltpu
from jax.sharding import PartitionSpec as P

MESH = pl.DeviceIdType.MESH
BF = jnp.bfloat16
F32 = jnp.float32
PAD = 4


def mm(a, b):
    return jnp.dot(a, b, preferred_element_type=F32)


def mm_nt(a, b):
    return lax.dot_general(a, b, (((1,), (1,)), ((), ())), preferred_element_type=F32)


def mm_tn(a, b):
    return lax.dot_general(a, b, (((0,), (0,)), ((), ())), preferred_element_type=F32)


def flip(tile):
    return tile.astype(F32).T.astype(BF)


def lay(parts):
    return parts[0] if len(parts) == 1 else jnp.concatenate(parts, axis=1)


def plan(orb, step):
    full = orb // step - 1
    cuts, start = [(i * step, step) for i in range(full)], full * step
    for length in (step // 2, step // 4, step // 8, step // 8):
        cuts.append((start, length))
        start += length
    return cuts


def kernel(
    chain, times, batch, step,
    ints, bmap, occ, virt, coul, cosine, out,
    own, own_rel, xbuf, side, diag_rel, stage, bm, mask, cos,
    occ_prev, occ_own, occ_edge, virt_prev, virt_own, virt_edge,
    l_side, w_prev, w_own, w_edge, coul_own, coul_left,
    acc, acc_diag, z_send, z_recv, z_side, z_edge, p_send, p_recv,
    load_sem, first_sem, own_sem, x_send, x_recv, edge_send, edge_recv, tile_send, tile_recv,
    coul_send, coul_recv, zs_send, zs_recv, hello, total, out_sem,
):
    aux, orb = ints.shape[0], ints.shape[1]
    part = aux // times
    col_blocks, row_blocks = bmap.shape
    width = orb // col_blocks
    group = aux // row_blocks
    pitch = orb + PAD
    me = lax.axis_index("orb")
    y = lax.axis_index("tm")
    right = lax.rem(me + 1, chain)
    left = lax.rem(me + chain - 1, chain)
    later = [lax.rem(y + d, times) for d in range(times)]
    before = [lax.rem(y + times - d, times) for d in range(times)]

    barrier = pltpu.get_barrier_semaphore()
    def load(src, dst, sem):
        copy = pltpu.make_async_copy(src, dst, sem)
        copy.start()
        return copy

    mine = pl.multiple_of(y * part, part)
    map_load = load(bmap, bm, load_sem.at[0])
    first_loads = []
    for i in range(orb // step):
        at = (pl.ds(mine, part), pl.ds(i * step, step))
        first_loads.append(load(ints.at[at], own.at[at], first_sem.at[i]))
    pl.semaphore_signal(barrier, inc=1, device_id=(left, y), device_id_type=MESH)
    for d in range(1, times):
        @pl.when(y + d < times)
        def _(d=d):
            pl.semaphore_signal(barrier, inc=1, device_id=(me, later[d]), device_id_type=MESH)

    own_loads = []
    for d in range(1, times):
        rows = pl.ds(pl.multiple_of(later[d] * part, part), part)
        own_loads.append(load(ints.at[rows], own.at[rows], own_sem.at[d]))
    tile_loads = []
    for k, (src, prev, mid) in enumerate(
        ((occ, occ_prev, occ_own), (virt, virt_prev, virt_own))
    ):
        tile_loads.append(load(src.at[0, :, pl.ds(0, orb)], prev.at[0], load_sem.at[1 + k]))
        tile_loads.append(load(src.at[0, :, pl.ds(orb, orb)], mid.at[0], load_sem.at[3 + k]))
    late_loads = [load(coul, coul_own, load_sem.at[5]), load(cosine, cos, load_sem.at[6])]

    pl.semaphore_wait(barrier, 1 + y)
    for d in range(1, times):
        @pl.when(y >= d)
        def _(d=d):
            pl.semaphore_signal(hello.at[d], inc=1, device_id=(me, before[d]), device_id_type=MESH)

    def remote(src, dst, s, r, where, peer):
        return pltpu.make_async_remote_copy(
            src_ref=src, dst_ref=dst, send_sem=s, recv_sem=r,
            device_id=(where, peer), device_id_type=MESH,
        )

    def send(*args):
        copy = remote(*args)
        copy.start()
        return copy

    edges = []
    for k, (src, dst) in enumerate(((occ, occ_edge), (virt, virt_edge))):
        edges.append(send(
            src.at[0, :, pl.ds(2 * orb, orb)], dst.at[0],
            edge_send.at[0, k], edge_recv.at[0, k], right, y,
        ))
    tiles = [[] for _ in range(times)]
    for d in range(1, times):
        for k, (src, dst, place) in enumerate((
            (occ, occ_own, 1), (virt, virt_own, 1), (occ, occ_prev, 0), (virt, virt_prev, 0),
        )):
            tiles[d].append(remote(
                src.at[0, :, pl.ds(place * orb, orb)], dst.at[d],
                tile_send.at[d, k], tile_recv.at[d, k], me, before[d],
            ))

        @pl.when(y >= d)
        def _(d=d):
            for copy in tiles[d]:
                copy.start()

    map_load.wait()
    values = bm[...].astype(F32)
    for r in range(row_blocks):
        for c in range(col_blocks):
            mask[r, pl.ds(c * width, width), :] = jnp.broadcast_to(
                values[c : c + 1, r : r + 1], (width, orb)
            ).astype(BF)

    def arrange(first, block):
        rows = pl.ds(pl.multiple_of(block, group), group)
        for g in range(part // group):
            at = pl.multiple_of(first + g * group, group)
            tile = own[pl.ds(at, group), rows, :] * mask[at // group, rows, :][None]
            own[pl.ds(at, group), rows, :] = tile
            own_rel[rows, pl.ds(at, group), :] = jnp.swapaxes(tile, 0, 1)

    slices = plan(orb, step)
    full = orb // step - 1

    def piece(start, length, i):
        rows = pl.ds(start, length)
        return remote(
            own_rel.at[rows, pl.ds(mine, part)], xbuf.at[rows],
            x_send.at[i], x_recv.at[i], right, y,
        )

    def first_part(i, carry):
        at = (pl.ds(mine, part), pl.ds(pl.multiple_of(i * step, step), step))
        pltpu.make_async_copy(ints.at[at], own.at[at], first_sem.at[i]).wait()
        for b in range(0, step, group):
            arrange(mine, i * step + b)
        piece(pl.multiple_of(i * step, step), step, i).start()
        return carry

    lax.fori_loop(0, full, first_part, 0)
    first_loads[full].wait()
    for b in range(0, step, group):
        arrange(mine, full * step + b)
    ends = len(slices) - 1
    keeps = jnp.logical_or(me < chain - 1, y == 0)
    lends = jnp.logical_and(me == chain - 1, y + 1 < times)
    last = pl.ds(*slices[ends])
    next_rows = pl.ds(pl.multiple_of(later[1 % times] * part, part), part)
    lent = remote(
        own_rel.at[last, next_rows], xbuf.at[last],
        x_send.at[ends + 1], x_recv.at[ends], right, later[1 % times],
    )
    for d in range(1, times):
        @pl.when(y < d)
        def _(d=d):
            pl.semaphore_wait(hello.at[times - d], 1)
            for copy in tiles[d]:
                copy.start()

    tiles = [copy for row in tiles for copy in row]
    for copy in own_loads:
        copy.wait()
    for d in range(1, times):
        base = pl.multiple_of(later[d] * part, part)

        def other_part(i, carry, base=base):
            arrange(base, i * group)
            return carry

        lax.fori_loop(0, orb // group, other_part, 0)

    @pl.when(lends)
    def _():
        lent.start()

    for i in range(full, ends):
        piece(*slices[i], i).start()

    @pl.when(keeps)
    def _():
        piece(*slices[ends], ends).start()

    couls = [send(coul, coul_left, coul_send, coul_recv, right, y)]

    def fold(i):
        span = 2 * group

        def body(j, carry):
            base = pl.multiple_of(j * span, span)
            for q in range(0, span, 2):
                x = jnp.concatenate([own[base + q], own[base + q + 1]], axis=1)
                g = mm(l_side[i], x)
                for k in range(2):
                    for c in range(2):
                        stage[k, pl.ds((q + c) * pitch, orb)] = g[
                            k * orb : (k + 1) * orb, c * orb : (c + 1) * orb
                        ]
            for k in range(2):
                for g in range(0, span, group):
                    at = pl.multiple_of((2 * i + k) * aux + base + g, group)
                    for m in range(orb):
                        side[m, pl.ds(at, group)] = stage[
                            k, pl.ds(g * pitch + m, group, stride=pitch), :
                        ].astype(BF)
            return carry

        lax.fori_loop(0, aux // span, body, 0)

    def sides(d, i):
        lanes = pl.ds(i * orb, orb)
        l_side[i, :orb] = flip(occ_prev[d])
        l_side[i, orb:] = occ_edge[d]
        w_prev[:, lanes] = flip(virt_prev[d])
        w_edge[:, lanes] = virt_edge[d]
        fold(i)

    for copy in tile_loads:
        copy.wait()
    for copy in edges:
        copy.wait_recv()
    passed = []
    for d in range(1, times):
        for k, where in enumerate((occ_edge, virt_edge)):
            passed.append(send(
                where.at[0], where.at[d], edge_send.at[d, k], edge_recv.at[d, k], me, before[d]
            ))
    sides(0, 0)

    for copy in tiles:
        copy.wait_recv()
    for d in range(times):
        w_own[:, pl.ds(d * orb, orb)] = flip(virt_own[d])

    some = min(part, 2 * group)

    def diagonal(i, carry):
        base = pl.multiple_of(mine + i * some, group)
        for quad in range(0, some, 4):
            x = own[pl.ds(base + quad, 4)]
            half = mm(x.reshape(4 * orb, orb), w_own[...]).astype(BF)
            for d in range(times):
                columns = [
                    half[q * orb : (q + 1) * orb, d * orb : (d + 1) * orb] for q in range(4)
                ]
                pair = mm(occ_own[d], jnp.concatenate(columns, axis=1))
                for q in range(4):
                    stage[d, pl.ds((quad + q) * pitch, orb)] = pair[:, q * orb : (q + 1) * orb]
        for d in range(times):
            for g in range(0, some, group):
                at = pl.multiple_of(d * part + i * some + g, group)
                for m in range(orb):
                    diag_rel[m, pl.ds(at, group)] = stage[
                        d, pl.ds(g * pitch + m, group, stride=pitch), :
                    ].astype(BF)
        return carry

    lax.fori_loop(0, part // some, diagonal, 0)

    acc_diag[...] = jnp.zeros_like(acc_diag)
    deep = step

    def respond_diag(i, carry):
        a = lay([diag_rel[i * deep + k] for k in range(deep)])
        b = lay([own_rel[i * deep + k] for k in range(deep)])
        acc_diag[...] += mm_nt(a, b)
        return carry

    lax.fori_loop(0, orb // deep, respond_diag, 0)
    for copy in late_loads:
        copy.wait()

    def weigh(e, read):
        total = cos[later[e], later[0]] * read(0)
        for d in range(1, times):
            total = total + cos[later[e], later[d]] * read(d)
        return total.astype(BF)

    diag_copies, z_copies, p_copies = [], [], []
    for e in range(times):
        z_send[e] = weigh(e, lambda d: acc_diag[pl.ds(d * part, part)])
        if e:
            diag_copies.append(send(
                z_send.at[e], z_recv.at[y], zs_send.at[0, e], zs_recv.at[0, e],
                me, later[e],
            ))
    z_recv[y] = z_send[0]

    acc[...] = jnp.zeros_like(acc)
    for first in range(0, times, batch):
        for i in range(batch):
            d = first + i
            if d:
                if d == 1:
                    for copy in passed:
                        copy.wait_recv()
                sides(d, i)

        def respond(start, length, kinds=(0, 1)):
            x = xbuf[pl.ds(start, length)].reshape(length * part, orb)
            for k in kinds:
                weights = (w_prev, w_edge)[k]
                half = mm(x, weights[...]).astype(BF)
                for i in range(batch):
                    a = lay([
                        half[j * part : (j + 1) * part, i * orb : (i + 1) * orb]
                        for j in range(length)
                    ])
                    b = lay([
                        side[start + j, pl.ds((2 * i + k) * aux, aux)] for j in range(length)
                    ])
                    acc[first + i, k] += mm_nt(a, b)

        def arrived(i, carry):
            if first == 0:
                piece(pl.multiple_of(i * step, step), step, i).wait_recv()
            respond(i * step, step)
            return carry

        lax.fori_loop(0, full, arrived, 0)
        for i in range(full, len(slices)):
            if first == 0:
                piece(*slices[i], i).wait_recv()
            closing = i == len(slices) - 1 and first + batch == times
            respond(*slices[i], kinds=(0,) if closing else (0, 1))

    for e in (*range(1, times), 0):
        z_side[e] = weigh(e, lambda d: acc[d, 0])
        if e:
            z_copies.append(send(
                z_side.at[e], z_edge.at[y], zs_send.at[1, e], zs_recv.at[1, e],
                me, later[e],
            ))
    respond(*slices[-1], kinds=(1,))
    for copy in diag_copies:
        copy.wait_recv()
    for e in range(times):
        panel = mm(weigh(e, lambda d: acc[d, 1]), coul_own[...])
        p_send[e] = panel.astype(BF)
        p_copies.append(send(
            p_send.at[e], p_recv.at[y], zs_send.at[2, e], zs_recv.at[2, e], left, later[e],
        ))
    total[...] = mm_tn(z_recv[...].reshape(aux, aux), coul_own[...])
    z_edge[y] = z_side[0]
    for copy in couls + z_copies + p_copies:
        copy.wait_recv()
    edge = mm_tn(z_edge[...].reshape(aux, aux), coul_left[...])
    total[...] += edge + p_recv[...].reshape(aux, out.shape[2]).astype(F32)
    stores = []
    for i in range(2):
        rows = pl.ds(i * (aux // 2), aux // 2)
        stores.append(load(total.at[rows], out.at[0, rows], out_sem.at[i]))
    for copy in tiles + edges + passed + couls + diag_copies + z_copies + p_copies:
        copy.wait_send()
    for i in range(ends):
        piece(*slices[i], i).wait_send()

    @pl.when(keeps)
    def _():
        piece(*slices[ends], ends).wait_send()

    @pl.when(lends)
    def _():
        lent.wait_send()

    for copy in stores:
        copy.wait()


def solution(mesh):
    chain, times = mesh.shape["orb"], mesh.shape["tm"]

    def body(integrals, block_map, green_occ, green_virt, coulomb, cosine):
        aux, orb = integrals.shape[0], integrals.shape[1]
        kw = coulomb.shape[1]
        part = aux // times
        group = aux // block_map.shape[0]
        step = orb // 4
        batch = 2 - times % 2
        count = len(plan(orb, step))
        any_space = pl.BlockSpec(memory_space=pl.ANY)
        dma = pltpu.SemaphoreType.DMA
        scratch = [
            pltpu.VMEM((aux, orb, orb), BF),
            pltpu.VMEM((orb, aux, orb), BF),
            pltpu.VMEM((orb, part, orb), BF),
            pltpu.VMEM((orb, 2 * batch * aux, orb), BF),
            pltpu.VMEM((orb, aux, orb), BF),
            pltpu.VMEM((max(2, times), (2 * group + 1) * (orb + PAD), orb), F32),
            pltpu.VMEM(block_map.shape[::-1], jnp.int32),
            pltpu.VMEM((block_map.shape[0], orb, orb), BF),
            pltpu.SMEM(cosine.shape, F32),
            *[pltpu.VMEM((times, orb, orb), BF)] * 6,
            pltpu.VMEM((batch, 2 * orb, orb), BF),
            pltpu.VMEM((orb, batch * orb), BF),
            pltpu.VMEM((orb, times * orb), BF),
            pltpu.VMEM((orb, batch * orb), BF),
            *[pltpu.VMEM((aux, kw), BF)] * 2,
            pltpu.VMEM((times, 2, part, aux), F32),
            pltpu.VMEM((aux, aux), F32),
            pltpu.VMEM((times, part, aux), BF),
            pltpu.VMEM((times, part, aux), BF),
            *[pltpu.VMEM((times, part, aux), BF)] * 2,
            *[pltpu.VMEM((times, part, kw), BF)] * 2,
            dma((7,)), dma((orb // step,)), dma((times,)),
            dma((count + 1,)), dma((count,)),
            dma((times, 2)), dma((times, 2)),
            dma((times, 4)), dma((times, 4)),
            dma, dma,
            dma((3, times)), dma((3, times)),
            pltpu.SemaphoreType.REGULAR((times,)),
            pltpu.VMEM((aux, kw), F32), dma((2,)),
        ]
        return pl.pallas_call(
            functools.partial(kernel, chain, times, batch, step),
            out_shape=jax.ShapeDtypeStruct((1, aux, kw), F32),
            in_specs=[any_space] * 6,
            out_specs=any_space,
            scratch_shapes=scratch,
            compiler_params=pltpu.CompilerParams(
                collective_id=0, has_side_effects=True, vmem_limit_bytes=56 * 2**20
            ),
        )(integrals, block_map.T, green_occ, green_virt, coulomb, cosine)

    in_specs = (
        P("orb", None, None),
        P("orb", None),
        P("tm", "orb", None),
        P("tm", "orb", None),
        P("orb", None),
        P(),
    )
    out_specs = P("tm", "orb", None)
    return jax.shard_map(body, mesh=mesh, in_specs=in_specs, out_specs=out_specs, check_vma=False)
```

```python
import functools

import jax
import jax.numpy as jnp
from jax import lax
from jax.experimental import pallas as pl
from jax.experimental.pallas import tpu as pltpu
from jax.sharding import PartitionSpec as P

MESH = pl.DeviceIdType.MESH
BF = jnp.bfloat16
F32 = jnp.float32
PAD = 4


def mm(a, b):
    return jnp.dot(a, b, preferred_element_type=F32)


def mm_nt(a, b):
    return lax.dot_general(a, b, (((1,), (1,)), ((), ())), preferred_element_type=F32)


def mm_tn(a, b):
    return lax.dot_general(a, b, (((0,), (0,)), ((), ())), preferred_element_type=F32)


def flip(tile):
    return tile.astype(F32).T.astype(BF)


def lay(parts):
    return parts[0] if len(parts) == 1 else jnp.concatenate(parts, axis=1)


def plan(orb, step):
    full = orb // step - 1
    cuts, start = [(i * step, step) for i in range(full)], full * step
    for length in (step // 2, step // 4, step // 8, step // 8):
        cuts.append((start, length))
        start += length
    return cuts


def kernel(
    chain, times, batch, step,
    ints, bmap, occ, virt, coul, cosine, out,
    own, own_rel, xbuf, side, diag_rel, stage, bm, mask, cos,
    occ_prev, occ_own, occ_edge, virt_prev, virt_own, virt_edge,
    l_side, w_prev, w_own, w_edge, coul_own, coul_left,
    acc, acc_diag, z_send, z_recv, z_side, z_edge, p_send, p_recv,
    load_sem, first_sem, own_sem, x_send, x_recv, edge_send, edge_recv, tile_send, tile_recv,
    coul_send, coul_recv, zs_send, zs_recv, hello, total, out_sem,
):
    aux, orb = ints.shape[0], ints.shape[1]
    part = aux // times
    col_blocks, row_blocks = bmap.shape
    width = orb // col_blocks
    group = aux // row_blocks
    pitch = orb + PAD
    me = lax.axis_index("orb")
    y = lax.axis_index("tm")
    right = lax.rem(me + 1, chain)
    left = lax.rem(me + chain - 1, chain)
    later = [lax.rem(y + d, times) for d in range(times)]
    before = [lax.rem(y + times - d, times) for d in range(times)]

    barrier = pltpu.get_barrier_semaphore()
    def load(src, dst, sem):
        copy = pltpu.make_async_copy(src, dst, sem)
        copy.start()
        return copy

    mine = pl.multiple_of(y * part, part)
    map_load = load(bmap, bm, load_sem.at[0])
    first_loads = []
    for i in range(orb // step):
        at = (pl.ds(mine, part), pl.ds(i * step, step))
        first_loads.append(load(ints.at[at], own.at[at], first_sem.at[i]))
    pl.semaphore_signal(barrier, inc=1, device_id=(left, y), device_id_type=MESH)
    for d in range(1, times):
        @pl.when(y + d < times)
        def _(d=d):
            pl.semaphore_signal(barrier, inc=1, device_id=(me, later[d]), device_id_type=MESH)

    own_loads = []
    for d in range(1, times):
        rows = pl.ds(pl.multiple_of(later[d] * part, part), part)
        own_loads.append(load(ints.at[rows], own.at[rows], own_sem.at[d]))
    tile_loads = []
    for k, (src, prev, mid) in enumerate(
        ((occ, occ_prev, occ_own), (virt, virt_prev, virt_own))
    ):
        tile_loads.append(load(src.at[0, :, pl.ds(0, orb)], prev.at[0], load_sem.at[1 + k]))
        tile_loads.append(load(src.at[0, :, pl.ds(orb, orb)], mid.at[0], load_sem.at[3 + k]))
    late_loads = [load(coul, coul_own, load_sem.at[5]), load(cosine, cos, load_sem.at[6])]

    pl.semaphore_wait(barrier, 1 + y)
    for d in range(1, times):
        @pl.when(y >= d)
        def _(d=d):
            pl.semaphore_signal(hello.at[d], inc=1, device_id=(me, before[d]), device_id_type=MESH)

    def remote(src, dst, s, r, where, peer):
        return pltpu.make_async_remote_copy(
            src_ref=src, dst_ref=dst, send_sem=s, recv_sem=r,
            device_id=(where, peer), device_id_type=MESH,
        )

    def send(*args):
        copy = remote(*args)
        copy.start()
        return copy

    edges = []
    for k, (src, dst) in enumerate(((occ, occ_edge), (virt, virt_edge))):
        edges.append(send(
            src.at[0, :, pl.ds(2 * orb, orb)], dst.at[0],
            edge_send.at[0, k], edge_recv.at[0, k], right, y,
        ))
    tiles = [[] for _ in range(times)]
    for d in range(1, times):
        for k, (src, dst, place) in enumerate((
            (occ, occ_own, 1), (virt, virt_own, 1), (occ, occ_prev, 0), (virt, virt_prev, 0),
        )):
            tiles[d].append(remote(
                src.at[0, :, pl.ds(place * orb, orb)], dst.at[d],
                tile_send.at[d, k], tile_recv.at[d, k], me, before[d],
            ))

        @pl.when(y >= d)
        def _(d=d):
            for copy in tiles[d]:
                copy.start()

    map_load.wait()
    values = bm[...].astype(F32)
    for r in range(row_blocks):
        for c in range(col_blocks):
            mask[r, pl.ds(c * width, width), :] = jnp.broadcast_to(
                values[c : c + 1, r : r + 1], (width, orb)
            ).astype(BF)

    def arrange(first, block):
        rows = pl.ds(pl.multiple_of(block, group), group)
        for g in range(part // group):
            at = pl.multiple_of(first + g * group, group)
            tile = own[pl.ds(at, group), rows, :] * mask[at // group, rows, :][None]
            own[pl.ds(at, group), rows, :] = tile
            own_rel[rows, pl.ds(at, group), :] = jnp.swapaxes(tile, 0, 1)

    slices = plan(orb, step)
    full = orb // step - 1

    def piece(start, length, i):
        rows = pl.ds(start, length)
        return remote(
            own_rel.at[rows, pl.ds(mine, part)], xbuf.at[rows],
            x_send.at[i], x_recv.at[i], right, y,
        )

    def first_part(i, carry):
        at = (pl.ds(mine, part), pl.ds(pl.multiple_of(i * step, step), step))
        pltpu.make_async_copy(ints.at[at], own.at[at], first_sem.at[i]).wait()
        for b in range(0, step, group):
            arrange(mine, i * step + b)
        piece(pl.multiple_of(i * step, step), step, i).start()
        return carry

    lax.fori_loop(0, full, first_part, 0)
    first_loads[full].wait()
    for b in range(0, step, group):
        arrange(mine, full * step + b)
    ends = len(slices) - 1
    keeps = jnp.logical_or(me < chain - 1, y == 0)
    lends = jnp.logical_and(me == chain - 1, y + 1 < times)
    last = pl.ds(*slices[ends])
    next_rows = pl.ds(pl.multiple_of(later[1 % times] * part, part), part)
    lent = remote(
        own_rel.at[last, next_rows], xbuf.at[last],
        x_send.at[ends + 1], x_recv.at[ends], right, later[1 % times],
    )
    for d in range(1, times):
        @pl.when(y < d)
        def _(d=d):
            pl.semaphore_wait(hello.at[times - d], 1)
            for copy in tiles[d]:
                copy.start()

    tiles = [copy for row in tiles for copy in row]
    for copy in own_loads:
        copy.wait()
    for d in range(1, times):
        base = pl.multiple_of(later[d] * part, part)

        def other_part(i, carry, base=base):
            arrange(base, i * group)
            return carry

        lax.fori_loop(0, orb // group, other_part, 0)

    @pl.when(lends)
    def _():
        lent.start()

    for i in range(full, ends):
        piece(*slices[i], i).start()

    @pl.when(keeps)
    def _():
        piece(*slices[ends], ends).start()

    couls = [send(coul, coul_left, coul_send, coul_recv, right, y)]

    def fold(i):
        span = 2 * group

        def body(j, carry):
            base = pl.multiple_of(j * span, span)
            for q in range(0, span, 2):
                x = jnp.concatenate([own[base + q], own[base + q + 1]], axis=1)
                g = mm(l_side[i], x)
                for k in range(2):
                    for c in range(2):
                        stage[k, pl.ds((q + c) * pitch, orb)] = g[
                            k * orb : (k + 1) * orb, c * orb : (c + 1) * orb
                        ]
            for k in range(2):
                for g in range(0, span, group):
                    at = pl.multiple_of((2 * i + k) * aux + base + g, group)
                    for m in range(orb):
                        side[m, pl.ds(at, group)] = stage[
                            k, pl.ds(g * pitch + m, group, stride=pitch), :
                        ].astype(BF)
            return carry

        lax.fori_loop(0, aux // span, body, 0)

    def sides(d, i):
        lanes = pl.ds(i * orb, orb)
        l_side[i, :orb] = flip(occ_prev[d])
        l_side[i, orb:] = occ_edge[d]
        w_prev[:, lanes] = flip(virt_prev[d])
        w_edge[:, lanes] = virt_edge[d]
        fold(i)

    for copy in tile_loads:
        copy.wait()
    for copy in edges:
        copy.wait_recv()
    passed = []
    for d in range(1, times):
        for k, where in enumerate((occ_edge, virt_edge)):
            passed.append(send(
                where.at[0], where.at[d], edge_send.at[d, k], edge_recv.at[d, k], me, before[d]
            ))
    sides(0, 0)

    for copy in tiles:
        copy.wait_recv()
    for d in range(times):
        w_own[:, pl.ds(d * orb, orb)] = flip(virt_own[d])

    some = min(part, 2 * group)

    def diagonal(i, carry):
        base = pl.multiple_of(mine + i * some, group)
        for quad in range(0, some, 4):
            x = own[pl.ds(base + quad, 4)]
            half = mm(x.reshape(4 * orb, orb), w_own[...]).astype(BF)
            for d in range(times):
                columns = [
                    half[q * orb : (q + 1) * orb, d * orb : (d + 1) * orb] for q in range(4)
                ]
                pair = mm(occ_own[d], jnp.concatenate(columns, axis=1))
                for q in range(4):
                    stage[d, pl.ds((quad + q) * pitch, orb)] = pair[:, q * orb : (q + 1) * orb]
        for d in range(times):
            for g in range(0, some, group):
                at = pl.multiple_of(d * part + i * some + g, group)
                for m in range(orb):
                    diag_rel[m, pl.ds(at, group)] = stage[
                        d, pl.ds(g * pitch + m, group, stride=pitch), :
                    ].astype(BF)
        return carry

    lax.fori_loop(0, part // some, diagonal, 0)

    acc_diag[...] = jnp.zeros_like(acc_diag)
    deep = step

    def respond_diag(i, carry):
        a = lay([diag_rel[i * deep + k] for k in range(deep)])
        b = lay([own_rel[i * deep + k] for k in range(deep)])
        acc_diag[...] += mm_nt(a, b)
        return carry

    lax.fori_loop(0, orb // deep, respond_diag, 0)
    for copy in late_loads:
        copy.wait()

    def weigh(e, read):
        total = cos[later[e], later[0]] * read(0)
        for d in range(1, times):
            total = total + cos[later[e], later[d]] * read(d)
        return total.astype(BF)

    diag_copies, z_copies, p_copies = [], [], []
    for e in range(times):
        z_send[e] = weigh(e, lambda d: acc_diag[pl.ds(d * part, part)])
        if e:
            diag_copies.append(send(
                z_send.at[e], z_recv.at[y], zs_send.at[0, e], zs_recv.at[0, e],
                me, later[e],
            ))
    z_recv[y] = z_send[0]

    acc[...] = jnp.zeros_like(acc)
    for first in range(0, times, batch):
        for i in range(batch):
            d = first + i
            if d:
                if d == 1:
                    for copy in passed:
                        copy.wait_recv()
                sides(d, i)

        def respond(start, length, kinds=(0, 1)):
            x = xbuf[pl.ds(start, length)].reshape(length * part, orb)
            for k in kinds:
                weights = (w_prev, w_edge)[k]
                half = mm(x, weights[...]).astype(BF)
                for i in range(batch):
                    a = lay([
                        half[j * part : (j + 1) * part, i * orb : (i + 1) * orb]
                        for j in range(length)
                    ])
                    b = lay([
                        side[start + j, pl.ds((2 * i + k) * aux, aux)] for j in range(length)
                    ])
                    acc[first + i, k] += mm_nt(a, b)

        def arrived(i, carry):
            if first == 0:
                piece(pl.multiple_of(i * step, step), step, i).wait_recv()
            respond(i * step, step)
            return carry

        lax.fori_loop(0, full, arrived, 0)
        for i in range(full, len(slices)):
            if first == 0:
                piece(*slices[i], i).wait_recv()
            closing = i == len(slices) - 1 and first + batch == times
            respond(*slices[i], kinds=(0,) if closing else (0, 1))

    for e in (*range(1, times), 0):
        z_side[e] = weigh(e, lambda d: acc[d, 0])
        if e:
            z_copies.append(send(
                z_side.at[e], z_edge.at[y], zs_send.at[1, e], zs_recv.at[1, e],
                me, later[e],
            ))
    respond(*slices[-1], kinds=(1,))
    for copy in diag_copies:
        copy.wait_recv()
    for e in range(times):
        panel = mm(weigh(e, lambda d: acc[d, 1]), coul_own[...])
        p_send[e] = panel.astype(BF)
        p_copies.append(send(
            p_send.at[e], p_recv.at[y], zs_send.at[2, e], zs_recv.at[2, e], left, later[e],
        ))
    total[...] = mm_tn(z_recv[...].reshape(aux, aux), coul_own[...])
    z_edge[y] = z_side[0]
    for copy in couls + z_copies + p_copies:
        copy.wait_recv()
    edge = z_edge[...].reshape(aux, aux)
    right_rows = p_recv[...].reshape(aux, out.shape[2])
    stores = []
    for i in range(2):
        first_row, half_rows = i * (aux // 2), aux // 2
        rows = pl.ds(first_row, half_rows)
        total[rows] += mm_tn(
            edge[:, first_row : first_row + half_rows], coul_left[...]
        ) + right_rows[first_row : first_row + half_rows].astype(F32)
        stores.append(load(total.at[rows], out.at[0, rows], out_sem.at[i]))
    for copy in tiles + edges + passed + couls + diag_copies + z_copies + p_copies:
        copy.wait_send()
    for i in range(ends):
        piece(*slices[i], i).wait_send()

    @pl.when(keeps)
    def _():
        piece(*slices[ends], ends).wait_send()

    @pl.when(lends)
    def _():
        lent.wait_send()

    for copy in stores:
        copy.wait()


def solution(mesh):
    chain, times = mesh.shape["orb"], mesh.shape["tm"]

    def body(integrals, block_map, green_occ, green_virt, coulomb, cosine):
        aux, orb = integrals.shape[0], integrals.shape[1]
        kw = coulomb.shape[1]
        part = aux // times
        group = aux // block_map.shape[0]
        step = orb // 4
        batch = 2 - times % 2
        count = len(plan(orb, step))
        any_space = pl.BlockSpec(memory_space=pl.ANY)
        dma = pltpu.SemaphoreType.DMA
        scratch = [
            pltpu.VMEM((aux, orb, orb), BF),
            pltpu.VMEM((orb, aux, orb), BF),
            pltpu.VMEM((orb, part, orb), BF),
            pltpu.VMEM((orb, 2 * batch * aux, orb), BF),
            pltpu.VMEM((orb, aux, orb), BF),
            pltpu.VMEM((max(2, times), (2 * group + 1) * (orb + PAD), orb), F32),
            pltpu.VMEM(block_map.shape[::-1], jnp.int32),
            pltpu.VMEM((block_map.shape[0], orb, orb), BF),
            pltpu.SMEM(cosine.shape, F32),
            *[pltpu.VMEM((times, orb, orb), BF)] * 6,
            pltpu.VMEM((batch, 2 * orb, orb), BF),
            pltpu.VMEM((orb, batch * orb), BF),
            pltpu.VMEM((orb, times * orb), BF),
            pltpu.VMEM((orb, batch * orb), BF),
            *[pltpu.VMEM((aux, kw), BF)] * 2,
            pltpu.VMEM((times, 2, part, aux), F32),
            pltpu.VMEM((aux, aux), F32),
            pltpu.VMEM((times, part, aux), BF),
            pltpu.VMEM((times, part, aux), BF),
            *[pltpu.VMEM((times, part, aux), BF)] * 2,
            *[pltpu.VMEM((times, part, kw), BF)] * 2,
            dma((7,)), dma((orb // step,)), dma((times,)),
            dma((count + 1,)), dma((count,)),
            dma((times, 2)), dma((times, 2)),
            dma((times, 4)), dma((times, 4)),
            dma, dma,
            dma((3, times)), dma((3, times)),
            pltpu.SemaphoreType.REGULAR((times,)),
            pltpu.VMEM((aux, kw), F32), dma((2,)),
        ]
        return pl.pallas_call(
            functools.partial(kernel, chain, times, batch, step),
            out_shape=jax.ShapeDtypeStruct((1, aux, kw), F32),
            in_specs=[any_space] * 6,
            out_specs=any_space,
            scratch_shapes=scratch,
            compiler_params=pltpu.CompilerParams(
                collective_id=0, has_side_effects=True, vmem_limit_bytes=56 * 2**20
            ),
        )(integrals, block_map.T, green_occ, green_virt, coulomb, cosine)

    in_specs = (
        P("orb", None, None),
        P("orb", None),
        P("tm", "orb", None),
        P("tm", "orb", None),
        P("orb", None),
        P(),
    )
    out_specs = P("tm", "orb", None)
    return jax.shard_map(body, mesh=mesh, in_specs=in_specs, out_specs=out_specs, check_vma=False)
```
